256 devices in a mesh: gx: 8 (over x, core), gy: 8 (over z), gz: 4 (over y).
Axes of the slice: x: 4, y: 4, z: 8, core: 2. Of those that a mesh axis runs over, the one named last changes fastest.
Arguments:
- gas: float32 [64, 32, 64, 512], P(None, 'gx', 'gy', 'gz'), may hold values from 0 to 1
- droplet: float32 [32, 64, 32768], P(None, None, ('gx', 'gy', 'gz')), may hold values from 0 to 1
- owner: int32 [32768, 1], P(('gx', 'gy', 'gz')), may hold values from 0 to 31; in each aligned block of 128 rows (0 to 127, 128 to 255, ...) at most 8 rows name the same one
- cells: int32 [8, 32768], P(None, ('gx', 'gy', 'gz')), may hold values from 0 to 4095
- weights: float32 [8, 32768], P(None, ('gx', 'gy', 'gz')), may hold values from 0.1 to 1
- mass: float32 [32768], P(('gx', 'gy', 'gz')), may hold values from 0.25 to 4
- liquid_rate: float32 [64], replicated, may hold values from 0.05 to 0.45
- surface_rate: float32 [64], replicated, may hold values from 0.05 to 0.5
- gas_rate: float32 [64], replicated, may hold values from 0.04 to 0.16
Outputs:
- gas_next: float32 [64, 32, 64, 512], P(None, 'gx', 'gy', 'gz')
- droplet_next: float32 [32, 64, 32768], P(None, None, ('gx', 'gy', 'gz'))
The draws below stay inside these ranges and needn't reach their ends.
Inputs may be any that keep to these rules, and one draw needn't show every extreme that they name: `owner`: among the 128 parcels of one device at most 8 name the same gas device, and some gas device is named by exactly 8 of them.
All inputs are finite; a program needn't handle non-finite values.
Results may differ from the reference program's by a relative error of at most 0.00002.
Values sent between devices are 32-bit elements; how exact they have to be, the bound alone decides.
A program may use at most 64 MiB of HBM per device.

```python
import math
import jax
import jax.numpy as jnp
import numpy as np

SPECIES = 64
NODES = 32
STENCIL = 8
DROP_STEPS = 4
GAS_STEPS = 2
CX = 4
CY = 8
CZ = 128
P_DEV = 128
CAP = 8
NX = 32
NY = 64
NZ = 512
PARCELS = 32768
N_GY = 8
N_GZ = 4


def with_ends(result, rng, least, largest):
    spot = [jax.random.randint(jax.random.fold_in(rng, axis), (), 0, length) for axis, length in enumerate(result.shape)]
    longest = result.shape.index(max(result.shape))
    beside = spot[:longest] + [(spot[longest] + 1) % result.shape[longest]] + spot[longest + 1:]
    return result.at[tuple(spot)].set(least).at[tuple(beside)].set(largest)


def shard_levels(own_key, extent, shards, smallest, largest):
    factor_of = 1.0
    for dim, shards_of in shards:
        draws = jax.random.uniform(jax.random.fold_in(jax.random.fold_in(own_key, 6), dim), (shards_of,), jnp.float32, smallest / len(shards), largest / len(shards))
        factor_of = factor_of * jnp.repeat(jnp.exp(draws), extent[dim] // shards_of).reshape((-1,) + (1,) * (len(extent) - 1 - dim))
    return factor_of


def routed_block(rng, own, number, rows, number_of, top, reach, skew):
    order = jax.random.permutation(rng, number_of)
    crowded, usual = shares(number_of, rows * top, reach, skew, True), shares(number_of, rows * top, reach, skew, False)
    places = jnp.arange(number_of)

    def named(sizes, turn):
        used = int((sizes > 0).sum())
        fixed = max(1, used // 4)
        passed = fixed + (places - fixed + turn * (used - fixed)) % max(1, number_of - fixed)
        return jnp.zeros((number_of,), jnp.int32).at[order[jnp.where(places < fixed, places, passed)]].set(jnp.asarray(sizes, jnp.int32))

    sizes = jnp.where(number % 4 == 0, named(crowded, number // 4), named(usual, number - number // 4 - 1))
    mixed = jax.random.permutation(jax.random.fold_in(own, 3), number_of)
    giver, sink = mixed[0:number_of // 2 * 2:2], mixed[1:number_of // 2 * 2:2]
    margin = jnp.minimum(sizes[giver] - 1, reach - sizes[sink]) // 2
    margin = jnp.where((giver == order[0]) | (sink == order[0]) | (sizes[sink] == 0), 0, jnp.maximum(margin, 0))
    passed = jax.random.randint(jax.random.fold_in(own, 4), (number_of // 2,), 0, 1 << 20) % (margin + 1)
    sizes = sizes.at[giver].add(-passed).at[sink].add(passed)
    items = jnp.searchsorted(jnp.cumsum(sizes), jnp.arange(rows * top), side="right").astype(jnp.int32)
    listing = items.reshape(top, rows).T
    listing = listing[jax.random.permutation(jax.random.fold_in(own, 1), rows)]
    turn = jax.random.randint(jax.random.fold_in(own, 2), (rows, 1), 0, top)
    return jnp.take_along_axis(listing, (jnp.arange(top)[None, :] + turn) % top, axis=1)


def shares(number_of, total, limit, lean, full):
    portions = [(1 << 20) // math.isqrt(grade ** lean) + 1 for grade in range(1, number_of + 1)]
    largest = limit if full else min(limit, max(-(-total // number_of), total * portions[0] // sum(portions)))
    least = 1 if total - largest >= number_of - 1 else 0
    counts, surplus = [largest] + [least] * (number_of - 1), total - largest - least * (number_of - 1)
    while surplus > 0:
        candidates = [i for i in range(1, number_of) if counts[i] < largest] or [i for i in range(1, number_of) if counts[i] < limit]
        whole, left = sum([portions[i] for i in candidates]), surplus
        for i in candidates:
            more = min(limit - counts[i], max(1, left * portions[i] // whole), surplus)
            counts[i] = counts[i] + more
            surplus = surplus - more
    return np.array(counts)


def setup_inputs(seed: int = 0) -> dict:
    key_list = jax.random.split(jax.random.key(seed), 10)
    gas = jnp.clip(1.0 * jax.random.uniform(key_list[0], (SPECIES, NX, NY, NZ), jnp.float32) ** shard_levels(key_list[0], (SPECIES, NX, NY, NZ), ((1, 8), (2, 8), (3, 4)), -0.2, 0.2), 0.0, 1.0)
    droplet = jnp.clip(1.0 * jax.random.uniform(key_list[1], (NODES, SPECIES, PARCELS), jnp.float32) ** shard_levels(key_list[1], (NODES, SPECIES, PARCELS), ((2, 256),), -0.2, 0.2), 0.0, 1.0)
    owner_keys = jax.random.split(jax.random.fold_in(key_list[2], 1), PARCELS // P_DEV)
    owner_turns = jax.random.permutation(jax.random.fold_in(key_list[2], 3), PARCELS // P_DEV)
    owner = jax.vmap(lambda own, number: routed_block(jax.random.fold_in(key_list[2], 2), own, number, P_DEV, N_GY * N_GZ, 1, CAP, 2))(owner_keys, owner_turns).reshape((PARCELS, 1))
    cells = with_ends(jax.random.randint(key_list[3], (STENCIL, PARCELS), 0, CX * CY * CZ), jax.random.fold_in(key_list[3], 1), 0, (CX * CY * CZ) - 1).astype(jnp.int32)
    weights = jnp.clip(0.1 + 0.9 * jax.random.uniform(key_list[4], (STENCIL, PARCELS), jnp.float32) ** shard_levels(key_list[4], (STENCIL, PARCELS), ((1, 256),), -0.2, 0.2), 0.1, 1.0)
    mass = jnp.clip(jnp.exp(math.log(4.0) - 2.7725887 * jax.random.uniform(key_list[5], (PARCELS,), jnp.float32) ** shard_levels(key_list[5], (PARCELS,), ((0, 256),), -0.2, 0.2)), 0.25, 4.0)
    liquid_rate = jnp.clip(jnp.exp(jax.random.uniform(key_list[6], (SPECIES,), jnp.float32, math.log(0.05), math.log(0.45))), 0.05, 0.45)
    surface_rate = jnp.clip(jnp.exp(jax.random.uniform(key_list[7], (SPECIES,), jnp.float32, math.log(0.05), math.log(0.5))), 0.05, 0.5)
    gas_rate = jnp.clip(jnp.exp(jax.random.uniform(key_list[8], (SPECIES,), jnp.float32, math.log(0.04), math.log(0.16))), 0.04, 0.16)
    return dict(gas=gas, droplet=droplet, owner=owner, cells=cells, weights=weights, mass=mass, liquid_rate=liquid_rate, surface_rate=surface_rate, gas_rate=gas_rate)


def droplet_steps(state, gas_at, liquid_rate, surface_rate):
    liquid_coef = liquid_rate[None, :, None]
    surface_coef = surface_rate[:, None]
    emitted = jnp.zeros(gas_at.shape, jnp.float32)
    for substep in range(DROP_STEPS):
        surface_flux = surface_coef * (state[-1] - gas_at)
        upper_node = jnp.concatenate([state[1:], state[-1:]], axis=0)
        lower_node = jnp.concatenate([state[1:2], state[:-1]], axis=0)
        state = state + liquid_coef * (upper_node - 2.0 * state + lower_node)
        state = state.at[-1].add(-surface_flux)
        emitted = emitted + surface_flux
    return state, emitted


def stencil_update(padded, field, gas_rate):
    beside = padded[:, 2:, 1:-1, 1:-1] + padded[:, :-2, 1:-1, 1:-1]
    beside = beside + padded[:, 1:-1, 2:, 1:-1] + padded[:, 1:-1, :-2, 1:-1]
    beside = beside + padded[:, 1:-1, 1:-1, 2:] + padded[:, 1:-1, 1:-1, :-2]
    return field + gas_rate[:, None, None, None] * (beside - 6.0 * field)


def reference(gas, droplet, owner, cells, weights, mass, liquid_rate, surface_rate, gas_rate):
    norm_wts = weights / jnp.sum(weights, axis=0, keepdims=True)
    parcel = jnp.arange(PARCELS, dtype=jnp.int32)
    slab_index = (parcel // P_DEV) // (N_GY * N_GZ)
    target = owner[:, 0]
    owner_row = target // N_GZ
    owner_col = target % N_GZ
    local_x = cells // (CY * CZ)
    local_y = (cells // CZ) % CY
    local_z = cells % CZ
    global_x = slab_index[None, :] * CX + local_x
    global_y = owner_row[None, :] * CY + local_y
    global_z = owner_col[None, :] * CZ + local_z
    global_cell = ((global_x * NY + global_y) * NZ + global_z).astype(jnp.int32)
    gasflat = gas.reshape(SPECIES, NX * NY * NZ)
    gas_at = jnp.zeros((SPECIES, PARCELS), jnp.float32)
    for corner in range(STENCIL):
        gas_at = gas_at + norm_wts[corner][None, :] * gasflat[:, global_cell[corner]]
    droplet_next, emitted = droplet_steps(droplet, gas_at, liquid_rate, surface_rate)
    source = mass[None, :] * emitted
    field = gas
    for substep in range(GAS_STEPS):
        padded = jnp.pad(field, ((0, 0), (1, 1), (1, 1), (1, 1)))
        field = stencil_update(padded, field, gas_rate)
    flat_out = field.reshape(SPECIES, NX * NY * NZ)
    for corner in range(STENCIL):
        flat_out = flat_out.at[:, global_cell[corner]].add(norm_wts[corner][None, :] * source)
    return flat_out.reshape(SPECIES, NX, NY, NZ), droplet_next
```

```python
import functools

import jax
import jax.numpy as jnp
from jax import lax
from jax.experimental import pallas as pl
from jax.experimental.pallas import tpu as pltpu
from jax.sharding import PartitionSpec as P

STENCIL = 8
DROP_STEPS = 4
MESH = pl.DeviceIdType.MESH
F32 = jnp.float32
BF16 = jnp.bfloat16
EXACT = lax.Precision.HIGHEST
NT = (((1,), (1,)), ((), ()))
NN = (((1,), (0,)), ((), ()))


def iota(shape, dim):
    return lax.broadcasted_iota(jnp.int32, shape, dim)


def column(row, lanes=None):
    n = row.shape[1]
    spread = jnp.broadcast_to(row, (n, n))
    picked = jnp.where(iota((n, n), 0) == iota((n, n), 1), spread, jnp.zeros_like(spread))
    return jnp.sum(picked, axis=1, keepdims=True)


def split(value):
    high = value.astype(BF16)
    low = (value - high.astype(F32)).astype(BF16)
    return high, low


def exact_dot(a, b, dims):
    return lax.dot_general(a, b, dims, precision=EXACT, preferred_element_type=F32)


def dot(a, b, dims):
    return lax.dot_general(a, b, dims, preferred_element_type=F32)


def kernel(
    n_gx, n_gy, n_gz, nx, ny,
    gas, droplet, owner, cells, weights, mass, liquid, surface, gasrate,
    gas_out, drop_out,
    raw, first, second, parts, drop, lam_b, sig_b, gam_b, reply_b, emit_b,
    w_hi, w_lo, zk_s, rk_s, vh_s, vl_s, acc_s, acc2_s, out_s,
    meta_send, meta_recv, base_send, base_recv, back_send, back_recv,
    edge_send, edge_recv,
    in_sem, out_sem,
    meta_ssem, meta_rsem, base_ssem, base_rsem, back_ssem, back_rsem,
    face_ssem, face_rsem,
):
    group = n_gy * n_gz
    rows = nx * ny
    half = 4 * group
    species = liquid.shape[1]
    nodes = droplet.shape[0]
    parcels = owner.shape[1]
    cz = 128

    gx = lax.axis_index("gx")
    gy = lax.axis_index("gy")
    gz = lax.axis_index("gz")
    me = gy * n_gz + gz

    def peer_id(o):
        return {"gy": o // n_gz, "gz": lax.rem(o, n_gz)}

    gas_in = pltpu.make_async_copy(gas, raw, in_sem.at[0])
    gas_in.start()
    drop_in = pltpu.make_async_copy(droplet, drop, in_sem.at[1])
    drop_in.start()

    barrier = pltpu.get_barrier_semaphore()

    def greet(j, carry):
        o = lax.rem(me + j, group)
        pl.semaphore_signal(barrier, inc=1, device_id=peer_id(o), device_id_type=MESH)
        return carry

    lax.fori_loop(1, group, greet, 0)
    for step in (1, n_gx - 1):
        pl.semaphore_signal(
            barrier, inc=1, device_id={"gx": lax.rem(gx + step, n_gx)}, device_id_type=MESH
        )

    own = owner[...]
    own_col = column(own)
    before = (own_col == own) & (iota((parcels, parcels), 0) < iota((parcels, parcels), 1))
    rank = jnp.sum(before.astype(F32), axis=0, keepdims=True).astype(jnp.int32)
    onehot = (iota((group, parcels), 0) == own).astype(F32)
    slot = (iota((8, parcels), 0) == rank).astype(F32)
    wts = weights[...]
    wts = wts / jnp.sum(wts, axis=0, keepdims=True)
    wts = wts * mass[...]
    cell = cells[...]
    cell_f = cell.astype(F32)
    tiles = [cell_f[q:q + 1] * slot for q in range(STENCIL)]
    tiles += [wts[q:q + 1] * slot for q in range(STENCIL)]
    spread = jnp.concatenate(tiles, axis=0)
    meta_send[...] = exact_dot(onehot, spread, NT)

    pl.semaphore_wait(barrier, group + 1)

    def exchange(src_of, dst_of, ssem, rsem):
        def send(j, carry):
            o = lax.rem(me + j, group)
            pltpu.make_async_remote_copy(
                src_ref=src_of(o), dst_ref=dst_of(me), send_sem=ssem.at[o], recv_sem=rsem.at[me],
                device_id=peer_id(o), device_id_type=MESH,
            ).start()
            return carry

        lax.fori_loop(1, group, send, 0)
        pltpu.make_async_copy(src_of(me), dst_of(me), rsem.at[me]).start()

    def await_recv(dst_of, rsem):
        def take(o, carry):
            pltpu.make_async_copy(dst_of(o), dst_of(o), rsem.at[o]).wait()
            return carry

        lax.fori_loop(0, group, take, 0)

    def await_send(src_of, ssem):
        def take(j, carry):
            o = lax.rem(me + j, group)
            pltpu.make_async_copy(src_of(o), src_of(o), ssem.at[o]).wait()
            return carry

        lax.fori_loop(1, group, take, 0)

    meta_row = lambda ref: (lambda o: ref.at[pl.ds(o, 1)])
    slab_row = lambda ref: (lambda o: ref.at[:, pl.ds(o, 1)])

    exchange(meta_row(meta_send), meta_row(meta_recv), meta_ssem, meta_rsem)

    def faces(buf, step):
        inner_x, inner_y = pl.ds(1, nx), pl.ds(1, ny)
        table = [
            (gx > 0, {"gx": gx - 1}, buf.at[1, inner_y], buf.at[nx + 1, inner_y], gx < n_gx - 1),
            (gx < n_gx - 1, {"gx": gx + 1}, buf.at[nx, inner_y], buf.at[0, inner_y], gx > 0),
            (gy > 0, {"gy": gy - 1}, buf.at[inner_x, 1], buf.at[inner_x, ny + 1], gy < n_gy - 1),
            (gy < n_gy - 1, {"gy": gy + 1}, buf.at[inner_x, ny], buf.at[inner_x, 0], gy > 0),
            (gz > 0, {"gz": gz - 1}, edge_send.at[step], edge_recv.at[step, 1], gz < n_gz - 1),
            (gz < n_gz - 1, {"gz": gz + 1}, edge_send.at[step], edge_recv.at[step, 0], gz > 0),
        ]
        out = []
        for i, (send_if, target, src, dst, recv_if) in enumerate(table):
            copy = pltpu.make_async_remote_copy(
                src_ref=src, dst_ref=dst, send_sem=face_ssem.at[step, i],
                recv_sem=face_rsem.at[step, i], device_id=target, device_id_type=MESH,
            )
            out.append((send_if, copy, recv_if, dst))
        return out

    def start_faces(buf, step):
        for send_if, copy, _, _ in faces(buf, step):
            pl.when(send_if)(copy.start)

    def await_faces(buf, step):
        for i, (_, _, recv_if, dst) in enumerate(faces(buf, step)):
            wait = pltpu.make_async_copy(dst, dst, face_rsem.at[step, i]).wait
            pl.when(recv_if)(wait)

    def drain_faces(buf, step):
        for send_if, copy, _, _ in faces(buf, step):
            pl.when(send_if)(copy.wait_send)

    def outside_zero(buf, step):
        zero_x = jnp.zeros((ny, species, cz), F32)
        zero_y = jnp.zeros((nx, species, cz), F32)
        zero_z = jnp.zeros((species, cz), F32)

        @pl.when(gx == 0)
        def _():
            buf[0, 1:ny + 1] = zero_x

        @pl.when(gx == n_gx - 1)
        def _():
            buf[nx + 1, 1:ny + 1] = zero_x

        @pl.when(gy == 0)
        def _():
            buf[1:nx + 1, 0] = zero_y

        @pl.when(gy == n_gy - 1)
        def _():
            buf[1:nx + 1, ny + 1] = zero_y

        @pl.when(gz == 0)
        def _():
            edge_recv[step, 0] = zero_z

        @pl.when(gz == n_gz - 1)
        def _():
            edge_recv[step, 1] = zero_z

    lane = iota((species, cz), 1)
    def edge_part(field, r):
        return jnp.where(lane // 2 == r, pltpu.roll(field, 2 * r + 1, 1), 0.0)

    gas_in.wait()

    def load_row(r, edges):
        field = raw[pl.ds(r, species, stride=rows), :]
        first[r // ny + 1, lax.rem(r, ny) + 1] = field
        high, low = split(field)
        pair, side = r // 2, lax.rem(r, 2)
        parts[pair, side, 0:species] = high
        parts[pair, side, species:2 * species] = low
        return edges + edge_part(field, r)

    edge_send[0] = lax.fori_loop(0, rows, load_row, jnp.zeros((species, cz), F32))
    start_faces(first, 0)
    outside_zero(first, 0)
    outside_zero(second, 1)

    lam_b[...] = jnp.broadcast_to(column(liquid[...]), (species, parcels))
    sig_b[...] = jnp.broadcast_to(column(surface[...]), (species, parcels))
    gam_b[...] = jnp.broadcast_to(column(gasrate[...]), (species, cz))
    drop_in.wait()

    def droplet_block(b, carry):
        at = pl.ds(pl.multiple_of(b * 8, 8), 8)
        lam, sig = lam_b[at], sig_b[at]
        state = drop[:, at]
        unit = jnp.zeros((DROP_STEPS, 8, parcels), F32)
        base = jnp.zeros((8, parcels), F32)
        answer = jnp.zeros((8, parcels), F32)
        for _ in range(DROP_STEPS):
            flux = sig * state[-1]
            upper = jnp.concatenate([state[1:], state[-1:]], axis=0)
            lower = jnp.concatenate([state[1:2], state[:-1]], axis=0)
            state = state + lam[None] * (upper - 2.0 * state + lower)
            state = jnp.concatenate([state[:-1], (state[-1] - flux)[None]], axis=0)
            base = base + flux
            flux = sig * (unit[-1] - 1.0)
            upper = jnp.concatenate([unit[1:], unit[-1:]], axis=0)
            lower = jnp.concatenate([jnp.zeros_like(unit[:1]), unit[:-1]], axis=0)
            unit = unit + lam[None] * (upper - 2.0 * unit + lower)
            unit = jnp.concatenate([unit[:-1], (unit[-1] - flux)[None]], axis=0)
            answer = answer + flux
        drop[:, at] = state
        reply_b[:, at] = unit
        emit_b[0, at] = base
        emit_b[1, at] = answer
        return carry

    lax.fori_loop(0, species // 8, droplet_block, 0)
    inner = pl.ds(0, nodes - DROP_STEPS)
    tail = pl.ds(nodes - DROP_STEPS, DROP_STEPS)
    drop_done = pltpu.make_async_copy(drop.at[inner], drop_out.at[inner], out_sem.at[0])
    drop_done.start()

    place = lax.rem(rank, 4) * group + own
    chosen = (iota((half, parcels), 0) == place).astype(F32)
    low_half = rank < 4
    base = emit_b[0]
    base = jnp.concatenate([jnp.where(low_half, base, 0.0), jnp.where(low_half, 0.0, base)], axis=0)
    base_send[...] = exact_dot(chosen, base, NT).reshape(4, group, 2 * species)
    exchange(slab_row(base_send), slab_row(base_recv), base_ssem, base_rsem)

    await_recv(meta_row(meta_recv), meta_rsem)
    table = meta_recv[...]
    lane_slot = lax.rem(iota((group, 128), 1), 8)
    stacked = jnp.concatenate([jnp.where(lane_slot == j, table, 0.0) for j in range(8)], axis=0)
    gather_q = (iota((16, 128), 1) // 8 == iota((16, 128), 0)).astype(F32)
    byslot = exact_dot(gather_q, stacked, NT)
    ids = (byslot[0:STENCIL] + 0.5).astype(jnp.int32)
    vals = byslot[STENCIL:]
    total = vals
    for turn in range(1, STENCIL):
        same = pltpu.roll(ids, turn, 0) == ids
        total = total + jnp.where(same, pltpu.roll(vals, turn, 0), 0.0)
    sum_v = jnp.sum(vals, axis=0, keepdims=True)
    inv_mass = jnp.where(sum_v > 0.0, 1.0 / jnp.where(sum_v > 0.0, sum_v, 1.0), 0.0)
    r_f = (ids // cz).astype(F32)
    z_f = lax.rem(ids, cz).astype(F32)
    v_high = total.astype(BF16).astype(F32)
    v_low = total - v_high
    for h in range(2):
        for k in range(STENCIL):
            for ref, val in ((zk_s, z_f), (rk_s, r_f), (vh_s, v_high), (vl_s, v_low)):
                one = val[k:k + 1, h * half:(h + 1) * half]
                ref[h, k] = jnp.broadcast_to(one, (16, half)).astype(BF16)

    zero = jnp.zeros((16, half), BF16)
    none = jnp.full((16, half), -1.0, BF16)

    def build(i, carry):
        h = lax.rem(i, 2)
        r = i // 2
        at_row = jnp.full((16, half), r.astype(F32)).astype(BF16)
        key = [jnp.where(rk_s[h, k] == at_row, zk_s[h, k], none) for k in range(STENCIL)]
        vh = [vh_s[h, k] for k in range(STENCIL)]
        vl = [vl_s[h, k] for k in range(STENCIL)]
        for chunk in range(cz // 16):
            z = (iota((16, half), 0) + chunk * 16).astype(F32).astype(BF16)
            high, low = zero, zero
            for k in reversed(range(STENCIL)):
                hit = key[k] == z
                high = jnp.where(hit, vh[k], high)
                low = jnp.where(hit, vl[k], low)
            w_hi[r, h, chunk * 16:chunk * 16 + 16] = high
            w_lo[r, h, chunk * 16:chunk * 16 + 16] = low
        return carry

    lax.fori_loop(0, 2 * rows, build, 0)

    def merged(step):
        up = edge_recv[step, 1]
        down = edge_recv[step, 0]
        even = lax.rem(lane, 2) == 0
        return jnp.where(even, pltpu.roll(up, cz - 1, 1), pltpu.roll(down, 1, 1))

    def stencil(buf, halo, r):
        x, y = r // ny + 1, lax.rem(r, ny) + 1
        mid = buf[x, y]
        beside = buf[x + 1, y] + buf[x - 1, y]
        beside = beside + buf[x, y + 1] + buf[x, y - 1]
        ends = pltpu.roll(halo, cz - 1 - 2 * r, 1)
        beside = beside + jnp.where(lane == cz - 1, ends, pltpu.roll(mid, cz - 1, 1))
        beside = beside + jnp.where(lane == 0, ends, pltpu.roll(mid, 1, 1))
        return mid + gam_b[...] * (beside - 6.0 * mid)

    await_faces(first, 0)
    halo = merged(0)

    def first_step(r, edges):
        field = stencil(first, halo, r)
        second[r // ny + 1, lax.rem(r, ny) + 1] = field
        return edges + edge_part(field, r)

    edge_send[1] = lax.fori_loop(0, rows, first_step, jnp.zeros((species, cz), F32))
    start_faces(second, 1)

    acc_s[...] = jnp.zeros_like(acc_s)
    acc2_s[...] = jnp.zeros_like(acc2_s)

    def gather(i, carry):
        lhs = jnp.concatenate([parts[i, 0], parts[i, 1]], axis=1)
        for h in range(2):
            at = slice(h * half, (h + 1) * half)
            hi = jnp.concatenate([w_hi[2 * i, h], w_hi[2 * i + 1, h]], axis=0)
            lo = jnp.concatenate([w_lo[2 * i, h], w_lo[2 * i + 1, h]], axis=0)
            acc_s[:, at] += dot(lhs, hi, NN)
            acc2_s[:, at] += dot(lhs[0:species], lo, NN)
        return carry

    lax.fori_loop(0, rows // 2, gather, 0)
    held = acc_s[0:species] + acc_s[species:] + acc2_s[...]
    gas_at = held * inv_mass
    back_send[...] = jnp.transpose(
        jnp.concatenate([gas_at[:, :half], gas_at[:, half:]], axis=0)
    ).reshape(4, group, 2 * species)
    exchange(slab_row(back_send), slab_row(back_recv), back_ssem, back_rsem)

    await_recv(slab_row(base_recv), base_rsem)
    got = jnp.transpose(base_recv[...].reshape(half, 2 * species))
    base = jnp.concatenate([got[0:species], got[species:]], axis=1)
    emitted = base + emit_b[1, :, 0:1] * gas_at
    high, low = split(emitted)
    both = jnp.concatenate([high, low], axis=0)

    await_faces(second, 1)
    halo2 = merged(1)

    def last_step(i, carry):
        hi = jnp.concatenate(
            [jnp.concatenate([w_hi[2 * i + s, 0], w_hi[2 * i + s, 1]], axis=1) for s in range(2)], axis=0
        )
        lo = jnp.concatenate(
            [jnp.concatenate([w_lo[2 * i + s, 0], w_lo[2 * i + s, 1]], axis=1) for s in range(2)], axis=0
        )
        one = dot(both, hi, NT)
        add = one[0:species] + one[species:] + dot(high, lo, NT)
        for s in range(2):
            r = 2 * i + s
            field = stencil(second, halo2, r) + add[:, s * cz:(s + 1) * cz]
            out_s[pl.ds(r, species, stride=rows), :] = field
        return carry

    lax.fori_loop(0, rows // 2, last_step, 0)
    gas_done = pltpu.make_async_copy(out_s, gas_out, out_sem.at[1])
    gas_done.start()

    await_recv(slab_row(back_recv), back_rsem)
    got = jnp.transpose(back_recv[...].reshape(half, 2 * species))
    seen = exact_dot(got, chosen, NN)
    seen = jnp.where(low_half, seen[0:species], seen[species:])
    for i in range(DROP_STEPS):
        drop[nodes - DROP_STEPS + i] = drop[nodes - DROP_STEPS + i] + reply_b[i] * seen
    tail_done = pltpu.make_async_copy(drop.at[tail], drop_out.at[tail], out_sem.at[2])
    tail_done.start()

    await_send(meta_row(meta_send), meta_ssem)
    await_send(slab_row(base_send), base_ssem)
    await_send(slab_row(back_send), back_ssem)
    drain_faces(first, 0)
    drain_faces(second, 1)
    drop_done.wait()
    gas_done.wait()
    tail_done.wait()


def on_device(gas, droplet, owner, cells, weights, mass, liquid_rate, surface_rate, gas_rate):
    n_gx, n_gy, n_gz = (lax.axis_size(a) for a in ("gx", "gy", "gz"))
    species, nx, ny, cz = gas.shape
    nodes, _, parcels = droplet.shape
    group = n_gy * n_gz
    rows = nx * ny
    half = 4 * group
    vmem = pl.BlockSpec(memory_space=pltpu.VMEM)
    anyw = pl.BlockSpec(memory_space=pl.ANY)
    dma = pltpu.SemaphoreType.DMA
    padded = pltpu.VMEM((nx + 2, ny + 2, species, cz), F32)
    slabs = pltpu.VMEM((4, group, 2 * species), F32)
    held = pltpu.VMEM((species, parcels), F32)
    onehot = pltpu.VMEM((rows, 2, cz, half), BF16)
    small = pltpu.VMEM((2, STENCIL, 16, half), BF16)
    gas_next, droplet_next = pl.pallas_call(
        functools.partial(kernel, n_gx, n_gy, n_gz, nx, ny),
        out_shape=(
            jax.ShapeDtypeStruct((species * rows, cz), F32),
            jax.ShapeDtypeStruct(droplet.shape, F32),
        ),
        in_specs=[anyw, anyw] + [vmem] * 7,
        out_specs=(anyw, anyw),
        scratch_shapes=[
            pltpu.VMEM((species * rows, cz), F32),
            padded, padded,
            pltpu.VMEM((rows // 2, 2, 2 * species, cz), BF16),
            pltpu.VMEM(droplet.shape, F32),
            held, held, pltpu.VMEM((species, cz), F32),
            pltpu.VMEM((DROP_STEPS, species, parcels), F32),
            pltpu.VMEM((2, species, parcels), F32),
            onehot, onehot, small, small, small, small,
            pltpu.VMEM((2 * species, 2 * half), F32),
            pltpu.VMEM((species, 2 * half), F32),
            pltpu.VMEM((species * rows, cz), F32),
            pltpu.VMEM((group, 128), F32), pltpu.VMEM((group, 128), F32),
            slabs, slabs, slabs, slabs,
            pltpu.VMEM((2, species, cz), F32), pltpu.VMEM((2, 2, species, cz), F32),
            dma((2,)), dma((3,)),
            dma((group,)), dma((group,)), dma((group,)), dma((group,)), dma((group,)), dma((group,)),
            dma((2, 6)), dma((2, 6)),
        ],
        compiler_params=pltpu.CompilerParams(
            collective_id=0, has_side_effects=True, vmem_limit_bytes=40 << 20
        ),
        name="spray",
    )(
        gas.reshape(species * rows, cz), droplet, owner.reshape(1, parcels), cells, weights,
        mass.reshape(1, parcels), liquid_rate.reshape(1, species), surface_rate.reshape(1, species),
        gas_rate.reshape(1, species),
    )
    return gas_next.reshape(gas.shape), droplet_next


def solution(mesh):
    return jax.shard_map(
        on_device,
        mesh=mesh,
        in_specs=(
            P(None, "gx", "gy", "gz"),
            P(None, None, ("gx", "gy", "gz")),
            P(("gx", "gy", "gz"), None),
            P(None, ("gx", "gy", "gz")),
            P(None, ("gx", "gy", "gz")),
            P(("gx", "gy", "gz")),
            P(),
            P(),
            P(),
        ),
        out_specs=(P(None, "gx", "gy", "gz"), P(None, None, ("gx", "gy", "gz"))),
        check_vma=False,
    )
```

```python
import functools

import jax
import jax.numpy as jnp
from jax import lax
from jax.experimental import pallas as pl
from jax.experimental.pallas import tpu as pltpu
from jax.sharding import PartitionSpec as P

STENCIL = 8
DROP_STEPS = 4
MESH = pl.DeviceIdType.MESH
F32 = jnp.float32
BF16 = jnp.bfloat16
EXACT = lax.Precision.HIGHEST
NT = (((1,), (1,)), ((), ()))
NN = (((1,), (0,)), ((), ()))


def iota(shape, dim):
    return lax.broadcasted_iota(jnp.int32, shape, dim)


def column(row, lanes=None):
    n = row.shape[1]
    spread = jnp.broadcast_to(row, (n, n))
    picked = jnp.where(iota((n, n), 0) == iota((n, n), 1), spread, jnp.zeros_like(spread))
    return jnp.sum(picked, axis=1, keepdims=True)


def split(value):
    high = value.astype(BF16)
    low = (value - high.astype(F32)).astype(BF16)
    return high, low


def exact_dot(a, b, dims):
    return lax.dot_general(a, b, dims, precision=EXACT, preferred_element_type=F32)


def dot(a, b, dims):
    return lax.dot_general(a, b, dims, preferred_element_type=F32)


def kernel(
    n_gx, n_gy, n_gz, nx, ny,
    gas, droplet, owner_in, cells_in, weights_in, mass_in, liquid_in, surface_in, gasrate_in,
    out_s, drop,
    owner, cells, weights, mass, liquid, surface, gasrate,
    raw, first, second, parts, lam_b, sig_b, gam_b, reply_b, emit_b,
    w_hi, w_lo, zk_s, rk_s, vh_s, vl_s, acc_s, acc2_s,
    meta_send, meta_recv, base_send, base_recv, back_send, back_recv,
    edge_send, edge_recv,
    in_sem, small_sem,
    meta_ssem, meta_rsem, base_ssem, base_rsem, back_ssem, back_rsem,
    face_ssem, face_rsem,
):
    group = n_gy * n_gz
    rows = nx * ny
    half = 4 * group
    species = liquid.shape[1]
    nodes = droplet.shape[0]
    parcels = owner.shape[1]
    cz = 128

    gx = lax.axis_index("gx")
    gy = lax.axis_index("gy")
    gz = lax.axis_index("gz")
    me = gy * n_gz + gz

    def peer_id(o):
        return {"gy": o // n_gz, "gz": lax.rem(o, n_gz)}

    smalls = [
        pltpu.make_async_copy(src, dst, small_sem.at[i])
        for i, (src, dst) in enumerate((
            (owner_in, owner), (cells_in, cells), (weights_in, weights), (mass_in, mass),
            (liquid_in, liquid), (surface_in, surface), (gasrate_in, gasrate),
        ))
    ]
    for copy in smalls:
        copy.start()
    gas_in = pltpu.make_async_copy(gas, raw, in_sem.at[0])
    gas_in.start()
    drop_in = pltpu.make_async_copy(droplet, drop, in_sem.at[1])
    drop_in.start()

    barrier = pltpu.get_barrier_semaphore()

    def greet(j, carry):
        o = lax.rem(me + j, group)
        pl.semaphore_signal(barrier, inc=1, device_id=peer_id(o), device_id_type=MESH)
        return carry

    lax.fori_loop(1, group, greet, 0)
    for step in (1, n_gx - 1):
        pl.semaphore_signal(
            barrier, inc=1, device_id={"gx": lax.rem(gx + step, n_gx)}, device_id_type=MESH
        )

    for copy in smalls:
        copy.wait()
    own = owner[...]
    own_col = column(own)
    before = (own_col == own) & (iota((parcels, parcels), 0) < iota((parcels, parcels), 1))
    rank = jnp.sum(before.astype(F32), axis=0, keepdims=True).astype(jnp.int32)
    onehot = (iota((group, parcels), 0) == own).astype(F32)
    slot = (iota((8, parcels), 0) == rank).astype(F32)
    wts = weights[...]
    wts = wts / jnp.sum(wts, axis=0, keepdims=True)
    wts = wts * mass[...]
    cell = cells[...]
    cell_f = cell.astype(F32)
    tiles = [cell_f[q:q + 1] * slot for q in range(STENCIL)]
    tiles += [wts[q:q + 1] * slot for q in range(STENCIL)]
    spread = jnp.concatenate(tiles, axis=0)
    meta_send[...] = exact_dot(onehot, spread, NT)

    pl.semaphore_wait(barrier, group + 1)

    def exchange(src_of, dst_of, ssem, rsem):
        def send(j, carry):
            o = lax.rem(me + j, group)
            pltpu.make_async_remote_copy(
                src_ref=src_of(o), dst_ref=dst_of(me), send_sem=ssem.at[o], recv_sem=rsem.at[me],
                device_id=peer_id(o), device_id_type=MESH,
            ).start()
            return carry

        lax.fori_loop(1, group, send, 0)
        pltpu.make_async_copy(src_of(me), dst_of(me), rsem.at[me]).start()

    def await_recv(dst_of, rsem):
        def take(o, carry):
            pltpu.make_async_copy(dst_of(o), dst_of(o), rsem.at[o]).wait()
            return carry

        lax.fori_loop(0, group, take, 0)

    def await_send(src_of, ssem):
        def take(j, carry):
            o = lax.rem(me + j, group)
            pltpu.make_async_copy(src_of(o), src_of(o), ssem.at[o]).wait()
            return carry

        lax.fori_loop(1, group, take, 0)

    meta_row = lambda ref: (lambda o: ref.at[pl.ds(o, 1)])
    slab_row = lambda ref: (lambda o: ref.at[:, pl.ds(o, 1)])

    exchange(meta_row(meta_send), meta_row(meta_recv), meta_ssem, meta_rsem)

    def faces(buf, step):
        inner_x, inner_y = pl.ds(1, nx), pl.ds(1, ny)
        table = [
            (gx > 0, {"gx": gx - 1}, buf.at[1, inner_y], buf.at[nx + 1, inner_y], gx < n_gx - 1),
            (gx < n_gx - 1, {"gx": gx + 1}, buf.at[nx, inner_y], buf.at[0, inner_y], gx > 0),
            (gy > 0, {"gy": gy - 1}, buf.at[inner_x, 1], buf.at[inner_x, ny + 1], gy < n_gy - 1),
            (gy < n_gy - 1, {"gy": gy + 1}, buf.at[inner_x, ny], buf.at[inner_x, 0], gy > 0),
            (gz > 0, {"gz": gz - 1}, edge_send.at[step], edge_recv.at[step, 1], gz < n_gz - 1),
            (gz < n_gz - 1, {"gz": gz + 1}, edge_send.at[step], edge_recv.at[step, 0], gz > 0),
        ]
        out = []
        for i, (send_if, target, src, dst, recv_if) in enumerate(table):
            copy = pltpu.make_async_remote_copy(
                src_ref=src, dst_ref=dst, send_sem=face_ssem.at[step, i],
                recv_sem=face_rsem.at[step, i], device_id=target, device_id_type=MESH,
            )
            out.append((send_if, copy, recv_if, dst))
        return out

    def start_faces(buf, step):
        for send_if, copy, _, _ in faces(buf, step):
            pl.when(send_if)(copy.start)

    def await_faces(buf, step):
        for i, (_, _, recv_if, dst) in enumerate(faces(buf, step)):
            wait = pltpu.make_async_copy(dst, dst, face_rsem.at[step, i]).wait
            pl.when(recv_if)(wait)

    def drain_faces(buf, step):
        for send_if, copy, _, _ in faces(buf, step):
            pl.when(send_if)(copy.wait_send)

    def outside_zero(buf, step):
        zero_x = jnp.zeros((ny, species, cz), F32)
        zero_y = jnp.zeros((nx, species, cz), F32)
        zero_z = jnp.zeros((species, cz), F32)

        @pl.when(gx == 0)
        def _():
            buf[0, 1:ny + 1] = zero_x

        @pl.when(gx == n_gx - 1)
        def _():
            buf[nx + 1, 1:ny + 1] = zero_x

        @pl.when(gy == 0)
        def _():
            buf[1:nx + 1, 0] = zero_y

        @pl.when(gy == n_gy - 1)
        def _():
            buf[1:nx + 1, ny + 1] = zero_y

        @pl.when(gz == 0)
        def _():
            edge_recv[step, 0] = zero_z

        @pl.when(gz == n_gz - 1)
        def _():
            edge_recv[step, 1] = zero_z

    lane = iota((species, cz), 1)
    def edge_part(field, r):
        return jnp.where(lane // 2 == r, pltpu.roll(field, 2 * r + 1, 1), 0.0)

    gas_in.wait()

    def load_rows(x, edges):
        for y in range(ny):
            r = x * ny + y
            field = raw[pl.ds(r, species, stride=rows), :]
            first[x + 1, y + 1] = field
            high, low = split(field)
            pair = x * (ny // 2) + y // 2
            parts[pair, y % 2, 0:species] = high
            parts[pair, y % 2, species:2 * species] = low
            edges = edges + edge_part(field, r)
        return edges

    edge_send[0] = lax.fori_loop(0, nx, load_rows, jnp.zeros((species, cz), F32))
    start_faces(first, 0)
    outside_zero(first, 0)
    outside_zero(second, 1)

    lam_b[...] = jnp.broadcast_to(column(liquid[...]), (species, parcels))
    sig_b[...] = jnp.broadcast_to(column(surface[...]), (species, parcels))
    gam_b[...] = jnp.broadcast_to(column(gasrate[...]), (species, cz))
    drop_in.wait()

    def droplet_block(b, carry):
        at = pl.ds(pl.multiple_of(b * 8, 8), 8)
        lam, sig = lam_b[at], sig_b[at]
        state = drop[:, at]
        unit = jnp.zeros((DROP_STEPS, 8, parcels), F32)
        base = jnp.zeros((8, parcels), F32)
        answer = jnp.zeros((8, parcels), F32)
        for _ in range(DROP_STEPS):
            flux = sig * state[-1]
            upper = jnp.concatenate([state[1:], state[-1:]], axis=0)
            lower = jnp.concatenate([state[1:2], state[:-1]], axis=0)
            state = state + lam[None] * (upper - 2.0 * state + lower)
            state = jnp.concatenate([state[:-1], (state[-1] - flux)[None]], axis=0)
            base = base + flux
            flux = sig * (unit[-1] - 1.0)
            upper = jnp.concatenate([unit[1:], unit[-1:]], axis=0)
            lower = jnp.concatenate([jnp.zeros_like(unit[:1]), unit[:-1]], axis=0)
            unit = unit + lam[None] * (upper - 2.0 * unit + lower)
            unit = jnp.concatenate([unit[:-1], (unit[-1] - flux)[None]], axis=0)
            answer = answer + flux
        drop[:, at] = state
        reply_b[:, at] = unit
        emit_b[0, at] = base
        emit_b[1, at] = answer
        return carry

    lax.fori_loop(0, species // 8, droplet_block, 0)
    place = lax.rem(rank, 4) * group + own
    chosen = (iota((half, parcels), 0) == place).astype(F32)
    low_half = rank < 4
    base = emit_b[0]
    base = jnp.concatenate([jnp.where(low_half, base, 0.0), jnp.where(low_half, 0.0, base)], axis=0)
    base_send[...] = exact_dot(chosen, base, NT).reshape(4, group, 2 * species)
    exchange(slab_row(base_send), slab_row(base_recv), base_ssem, base_rsem)

    await_recv(meta_row(meta_recv), meta_rsem)
    table = meta_recv[...]
    lane_slot = lax.rem(iota((group, 128), 1), 8)
    stacked = jnp.concatenate([jnp.where(lane_slot == j, table, 0.0) for j in range(8)], axis=0)
    gather_q = (iota((16, 128), 1) // 8 == iota((16, 128), 0)).astype(F32)
    byslot = exact_dot(gather_q, stacked, NT)
    ids = (byslot[0:STENCIL] + 0.5).astype(jnp.int32)
    vals = byslot[STENCIL:]
    total = vals
    for turn in range(1, STENCIL):
        same = pltpu.roll(ids, turn, 0) == ids
        total = total + jnp.where(same, pltpu.roll(vals, turn, 0), 0.0)
    sum_v = jnp.sum(vals, axis=0, keepdims=True)
    inv_mass = jnp.where(sum_v > 0.0, 1.0 / jnp.where(sum_v > 0.0, sum_v, 1.0), 0.0)
    r_f = (ids // cz).astype(F32)
    z_f = lax.rem(ids, cz).astype(F32)
    v_high = total.astype(BF16).astype(F32)
    v_low = total - v_high
    for h in range(2):
        for k in range(STENCIL):
            for ref, val in ((zk_s, z_f), (rk_s, r_f), (vh_s, v_high), (vl_s, v_low)):
                one = val[k:k + 1, h * half:(h + 1) * half]
                ref[h, k] = jnp.broadcast_to(one, (8, half))

    zero = jnp.zeros((16, half), BF16)

    def twice(value):
        return jnp.concatenate([value, value], axis=0).astype(BF16)

    def build(i, carry):
        h = lax.rem(i, 2)
        r = i // 2
        at_row = jnp.full((8, half), r.astype(F32))
        key = [twice(jnp.where(rk_s[h, k] == at_row, zk_s[h, k], -1.0)) for k in range(STENCIL)]
        vh = [twice(vh_s[h, k]) for k in range(STENCIL)]
        vl = [twice(vl_s[h, k]) for k in range(STENCIL)]
        for chunk in range(cz // 16):
            z = (iota((16, half), 0) + chunk * 16).astype(F32).astype(BF16)
            high, low = zero, zero
            for k in reversed(range(STENCIL)):
                hit = key[k] == z
                high = jnp.where(hit, vh[k], high)
                low = jnp.where(hit, vl[k], low)
            w_hi[r, h, chunk * 16:chunk * 16 + 16] = high
            w_lo[r, h, chunk * 16:chunk * 16 + 16] = low
        return carry

    lax.fori_loop(0, 2 * rows, build, 0)

    def merged(step):
        up = edge_recv[step, 1]
        down = edge_recv[step, 0]
        even = lax.rem(lane, 2) == 0
        return jnp.where(even, pltpu.roll(up, cz - 1, 1), pltpu.roll(down, 1, 1))

    def stencil(buf, halo, x, y):
        r = x * ny + y
        x, y = x + 1, y + 1
        mid = buf[x, y]
        beside = buf[x + 1, y] + buf[x - 1, y]
        beside = beside + buf[x, y + 1] + buf[x, y - 1]
        ends = pltpu.roll(halo, cz - 1 - 2 * r, 1)
        beside = beside + jnp.where(lane == cz - 1, ends, pltpu.roll(mid, cz - 1, 1))
        beside = beside + jnp.where(lane == 0, ends, pltpu.roll(mid, 1, 1))
        return mid + gam_b[...] * (beside - 6.0 * mid)

    await_faces(first, 0)
    halo = merged(0)

    def first_step(x, edges):
        for y in range(ny):
            field = stencil(first, halo, x, y)
            second[x + 1, y + 1] = field
            edges = edges + edge_part(field, x * ny + y)
        return edges

    edge_send[1] = lax.fori_loop(0, nx, first_step, jnp.zeros((species, cz), F32))
    start_faces(second, 1)

    acc_s[...] = jnp.zeros_like(acc_s)
    acc2_s[...] = jnp.zeros_like(acc2_s)

    def gather(g, carry):
        for h in range(2):
            at = slice(h * half, (h + 1) * half)
            one, two = acc_s[:, at], acc2_s[:, at]
            for k in range(4):
                i = 4 * g + k
                lhs = jnp.concatenate([parts[i, 0], parts[i, 1]], axis=1)
                hi = jnp.concatenate([w_hi[2 * i, h], w_hi[2 * i + 1, h]], axis=0)
                lo = jnp.concatenate([w_lo[2 * i, h], w_lo[2 * i + 1, h]], axis=0)
                one = one + dot(lhs, hi, NN)
                two = two + dot(lhs[0:species], lo, NN)
            acc_s[:, at] = one
            acc2_s[:, at] = two
        return carry

    lax.fori_loop(0, rows // 8, gather, 0)
    held = acc_s[0:species] + acc_s[species:] + acc2_s[...]
    gas_at = held * inv_mass
    back_send[...] = jnp.transpose(
        jnp.concatenate([gas_at[:, :half], gas_at[:, half:]], axis=0)
    ).reshape(4, group, 2 * species)
    exchange(slab_row(back_send), slab_row(back_recv), back_ssem, back_rsem)

    await_recv(slab_row(base_recv), base_rsem)
    got = jnp.transpose(base_recv[...].reshape(half, 2 * species))
    base = jnp.concatenate([got[0:species], got[species:]], axis=1)
    emitted = base + emit_b[1, :, 0:1] * gas_at
    high, low = split(emitted)
    both = jnp.concatenate([high, low], axis=0)

    await_faces(second, 1)
    halo2 = merged(1)

    def last_step(x, carry):
        for k in range(ny // 2):
            i = x * (ny // 2) + k
            hi = jnp.concatenate(
                [jnp.concatenate([w_hi[2 * i + t, 0], w_hi[2 * i + t, 1]], axis=1) for t in range(2)], axis=0
            )
            lo = jnp.concatenate(
                [jnp.concatenate([w_lo[2 * i + t, 0], w_lo[2 * i + t, 1]], axis=1) for t in range(2)], axis=0
            )
            one = dot(both, hi, NT)
            add = one[0:species] + one[species:] + dot(high, lo, NT)
            for t in range(2):
                field = stencil(second, halo2, x, 2 * k + t) + add[:, t * cz:(t + 1) * cz]
                out_s[pl.ds(2 * i + t, species, stride=rows), :] = field
        return carry

    lax.fori_loop(0, nx, last_step, 0)

    await_recv(slab_row(back_recv), back_rsem)
    got = jnp.transpose(back_recv[...].reshape(half, 2 * species))
    seen = exact_dot(got, chosen, NN)
    seen = jnp.where(low_half, seen[0:species], seen[species:])
    for i in range(DROP_STEPS):
        drop[nodes - DROP_STEPS + i] = drop[nodes - DROP_STEPS + i] + reply_b[i] * seen

    await_send(meta_row(meta_send), meta_ssem)
    await_send(slab_row(base_send), base_ssem)
    await_send(slab_row(back_send), back_ssem)
    drain_faces(first, 0)
    drain_faces(second, 1)


def on_device(gas, droplet, owner, cells, weights, mass, liquid_rate, surface_rate, gas_rate):
    n_gx, n_gy, n_gz = (lax.axis_size(a) for a in ("gx", "gy", "gz"))
    species, nx, ny, cz = gas.shape
    nodes, _, parcels = droplet.shape
    group = n_gy * n_gz
    rows = nx * ny
    half = 4 * group
    vmem = pl.BlockSpec(memory_space=pltpu.VMEM)
    hbm = pl.BlockSpec(memory_space=pltpu.MemorySpace.HBM)
    dma = pltpu.SemaphoreType.DMA
    padded = pltpu.VMEM((nx + 2, ny + 2, species, cz), F32)
    slabs = pltpu.VMEM((4, group, 2 * species), F32)
    held = pltpu.VMEM((species, parcels), F32)
    onehot = pltpu.VMEM((rows, 2, cz, half), BF16)
    small = pltpu.VMEM((2, STENCIL, 8, half), F32)
    gas_next, droplet_next = pl.pallas_call(
        functools.partial(kernel, n_gx, n_gy, n_gz, nx, ny),
        out_shape=(
            jax.ShapeDtypeStruct((species * rows, cz), F32),
            jax.ShapeDtypeStruct(droplet.shape, F32),
        ),
        in_specs=[hbm] * 9,
        out_specs=(vmem, vmem),
        scratch_shapes=[
            pltpu.VMEM((1, parcels), jnp.int32), pltpu.VMEM((STENCIL, parcels), jnp.int32),
            pltpu.VMEM((STENCIL, parcels), F32), pltpu.VMEM((1, parcels), F32),
            pltpu.VMEM((1, species), F32), pltpu.VMEM((1, species), F32), pltpu.VMEM((1, species), F32),
            pltpu.VMEM((species * rows, cz), F32),
            padded, padded,
            pltpu.VMEM((rows // 2, 2, 2 * species, cz), BF16),
            held, held, pltpu.VMEM((species, cz), F32),
            pltpu.VMEM((DROP_STEPS, species, parcels), F32),
            pltpu.VMEM((2, species, parcels), F32),
            onehot, onehot, small, small, small, small,
            pltpu.VMEM((2 * species, 2 * half), F32),
            pltpu.VMEM((species, 2 * half), F32),
            pltpu.VMEM((group, 128), F32), pltpu.VMEM((group, 128), F32),
            slabs, slabs, slabs, slabs,
            pltpu.VMEM((2, species, cz), F32), pltpu.VMEM((2, 2, species, cz), F32),
            dma((2,)), dma((7,)),
            dma((group,)), dma((group,)), dma((group,)), dma((group,)), dma((group,)), dma((group,)),
            dma((2, 6)), dma((2, 6)),
        ],
        compiler_params=pltpu.CompilerParams(
            collective_id=0, has_side_effects=True, vmem_limit_bytes=40 << 20
        ),
        name="spray",
    )(*(
        pltpu.with_memory_space_constraint(a, pltpu.MemorySpace.HBM)
        for a in (
            gas.reshape(species * rows, cz), droplet, owner.reshape(1, parcels), cells, weights,
            mass.reshape(1, parcels), liquid_rate.reshape(1, species), surface_rate.reshape(1, species),
            gas_rate.reshape(1, species),
        )
    ))
    return gas_next.reshape(gas.shape), droplet_next


def solution(mesh):
    return jax.shard_map(
        on_device,
        mesh=mesh,
        in_specs=(
            P(None, "gx", "gy", "gz"),
            P(None, None, ("gx", "gy", "gz")),
            P(("gx", "gy", "gz"), None),
            P(None, ("gx", "gy", "gz")),
            P(None, ("gx", "gy", "gz")),
            P(("gx", "gy", "gz")),
            P(),
            P(),
            P(),
        ),
        out_specs=(P(None, "gx", "gy", "gz"), P(None, None, ("gx", "gy", "gz"))),
        check_vma=False,
    )
```

```python
import functools

import jax
import jax.numpy as jnp
from jax import lax
from jax.experimental import pallas as pl
from jax.experimental.pallas import tpu as pltpu
from jax.sharding import PartitionSpec as P

STENCIL = 8
DROP_STEPS = 4
MESH = pl.DeviceIdType.MESH
F32 = jnp.float32
BF16 = jnp.bfloat16
EXACT = lax.Precision.HIGHEST
NT = (((1,), (1,)), ((), ()))
NN = (((1,), (0,)), ((), ()))


def iota(shape, dim):
    return lax.broadcasted_iota(jnp.int32, shape, dim)


def column(row, lanes=None):
    n = row.shape[1]
    spread = jnp.broadcast_to(row, (n, n))
    picked = jnp.where(iota((n, n), 0) == iota((n, n), 1), spread, jnp.zeros_like(spread))
    return jnp.sum(picked, axis=1, keepdims=True)


def split(value):
    high = value.astype(BF16)
    low = (value - high.astype(F32)).astype(BF16)
    return high, low


def exact_dot(a, b, dims):
    return lax.dot_general(a, b, dims, precision=EXACT, preferred_element_type=F32)


def dot(a, b, dims):
    return lax.dot_general(a, b, dims, preferred_element_type=F32)


def kernel(
    n_gx, n_gy, n_gz, nx, ny,
    gas, droplet, owner_in, cells_in, weights_in, mass_in, liquid_in, surface_in, gasrate_in,
    out_s, drop,
    owner, cells, weights, mass, liquid, surface, gasrate,
    raw, first, second, parts, lam_b, sig_b, gam_b, reply_b, emit_b,
    w_hi, w_lo, zk_s, rk_s, vh_s, vl_s, acc_s, acc2_s,
    meta_send, meta_recv, base_send, base_recv, back_send, back_recv,
    edge_send, edge_recv,
    in_sem, small_sem,
    meta_ssem, meta_rsem, base_ssem, base_rsem, back_ssem, back_rsem,
    face_ssem, face_rsem,
):
    group = n_gy * n_gz
    rows = nx * ny
    half = 4 * group
    species = liquid.shape[1]
    nodes = droplet.shape[0]
    parcels = owner.shape[1]
    cz = 128

    gx = lax.axis_index("gx")
    gy = lax.axis_index("gy")
    gz = lax.axis_index("gz")
    me = gy * n_gz + gz

    shifted_z = [lax.rem(gz + b, n_gz) for b in range(n_gz)]

    def each_peer(act):
        def turn(a, carry):
            to_y = lax.rem(gy + a, n_gy)
            for b in range(n_gz):
                to_z = shifted_z[b]
                run = functools.partial(act, to_y * n_gz + to_z, {"gy": to_y, "gz": to_z})
                if b == 0:
                    pl.when(a > 0)(run)
                else:
                    run()
            return carry

        lax.fori_loop(0, n_gy, turn, 0)

    smalls = [
        pltpu.make_async_copy(src, dst, small_sem.at[i])
        for i, (src, dst) in enumerate((
            (owner_in, owner), (cells_in, cells), (weights_in, weights), (mass_in, mass),
            (liquid_in, liquid), (surface_in, surface), (gasrate_in, gasrate),
        ))
    ]
    for copy in smalls:
        copy.start()
    gas_in = pltpu.make_async_copy(gas, raw, in_sem.at[0])
    gas_in.start()
    drop_in = pltpu.make_async_copy(droplet, drop, in_sem.at[1])
    drop_in.start()

    barrier = pltpu.get_barrier_semaphore()

    each_peer(lambda o, where: pl.semaphore_signal(
        barrier, inc=1, device_id=where, device_id_type=MESH
    ))
    for step in (1, n_gx - 1):
        pl.semaphore_signal(
            barrier, inc=1, device_id={"gx": lax.rem(gx + step, n_gx)}, device_id_type=MESH
        )

    for copy in smalls:
        copy.wait()
    own = owner[...]
    own_col = column(own)
    before = (own_col == own) & (iota((parcels, parcels), 0) < iota((parcels, parcels), 1))
    rank = jnp.sum(before.astype(F32), axis=0, keepdims=True).astype(jnp.int32)
    onehot = (iota((group, parcels), 0) == own).astype(F32)
    slot = (iota((8, parcels), 0) == rank).astype(F32)
    wts = weights[...]
    wts = wts / jnp.sum(wts, axis=0, keepdims=True)
    wts = wts * mass[...]
    cell = cells[...]
    cell_f = cell.astype(F32)
    tiles = [cell_f[q:q + 1] * slot for q in range(STENCIL)]
    tiles += [wts[q:q + 1] * slot for q in range(STENCIL)]
    spread = jnp.concatenate(tiles, axis=0)
    meta_send[...] = exact_dot(onehot, spread, NT)

    pl.semaphore_wait(barrier, group + 1)

    def exchange(src_of, dst_of, ssem, rsem):
        each_peer(lambda o, where: pltpu.make_async_remote_copy(
            src_ref=src_of(o), dst_ref=dst_of(me), send_sem=ssem, recv_sem=rsem,
            device_id=where, device_id_type=MESH,
        ).start())
        pltpu.make_async_copy(src_of(me), dst_of(me), rsem).start()

    def await_all(ref, sem):
        pltpu.make_async_copy(ref, ref, sem).wait()

    most = pl.ds(0, group - 1)

    meta_row = lambda ref: (lambda o: ref.at[pl.ds(o, 1)])
    slab_row = lambda ref: (lambda o: ref.at[:, pl.ds(o, 1)])

    exchange(meta_row(meta_send), meta_row(meta_recv), meta_ssem, meta_rsem)

    def faces(buf, step):
        inner_x, inner_y = pl.ds(1, nx), pl.ds(1, ny)
        table = [
            (gx > 0, {"gx": gx - 1}, buf.at[1, inner_y], buf.at[nx + 1, inner_y], gx < n_gx - 1),
            (gx < n_gx - 1, {"gx": gx + 1}, buf.at[nx, inner_y], buf.at[0, inner_y], gx > 0),
            (gy > 0, {"gy": gy - 1}, buf.at[inner_x, 1], buf.at[inner_x, ny + 1], gy < n_gy - 1),
            (gy < n_gy - 1, {"gy": gy + 1}, buf.at[inner_x, ny], buf.at[inner_x, 0], gy > 0),
            (gz > 0, {"gz": gz - 1}, edge_send.at[step], edge_recv.at[step, 1], gz < n_gz - 1),
            (gz < n_gz - 1, {"gz": gz + 1}, edge_send.at[step], edge_recv.at[step, 0], gz > 0),
        ]
        out = []
        for i, (send_if, target, src, dst, recv_if) in enumerate(table):
            copy = pltpu.make_async_remote_copy(
                src_ref=src, dst_ref=dst, send_sem=face_ssem.at[step, i],
                recv_sem=face_rsem.at[step, i], device_id=target, device_id_type=MESH,
            )
            out.append((send_if, copy, recv_if, dst))
        return out

    def start_faces(buf, step):
        for send_if, copy, _, _ in faces(buf, step):
            pl.when(send_if)(copy.start)

    def await_faces(buf, step):
        for i, (_, _, recv_if, dst) in enumerate(faces(buf, step)):
            wait = pltpu.make_async_copy(dst, dst, face_rsem.at[step, i]).wait
            pl.when(recv_if)(wait)

    def drain_faces(buf, step):
        for send_if, copy, _, _ in faces(buf, step):
            pl.when(send_if)(copy.wait_send)

    def outside_zero(buf, step):
        zero_x = jnp.zeros((ny, species, cz), F32)
        zero_y = jnp.zeros((nx, species, cz), F32)
        zero_z = jnp.zeros((species, cz), F32)

        @pl.when(gx == 0)
        def _():
            buf[0, 1:ny + 1] = zero_x

        @pl.when(gx == n_gx - 1)
        def _():
            buf[nx + 1, 1:ny + 1] = zero_x

        @pl.when(gy == 0)
        def _():
            buf[1:nx + 1, 0] = zero_y

        @pl.when(gy == n_gy - 1)
        def _():
            buf[1:nx + 1, ny + 1] = zero_y

        @pl.when(gz == 0)
        def _():
            edge_recv[step, 0] = zero_z

        @pl.when(gz == n_gz - 1)
        def _():
            edge_recv[step, 1] = zero_z

    lane = iota((species, cz), 1)
    def edge_part(field, r):
        return jnp.where(lane // 2 == r, pltpu.roll(field, 2 * r + 1, 1), 0.0)

    gas_in.wait()

    def load_rows(x, edges):
        for y in range(ny):
            r = x * ny + y
            field = raw[pl.ds(r, species, stride=rows), :]
            first[x + 1, y + 1] = field
            high, low = split(field)
            pair = x * (ny // 2) + y // 2
            parts[pair, y % 2, 0:species] = high
            parts[pair, y % 2, species:2 * species] = low
            edges = edges + edge_part(field, r)
        return edges

    edge_send[0] = lax.fori_loop(0, nx, load_rows, jnp.zeros((species, cz), F32))
    start_faces(first, 0)
    outside_zero(first, 0)
    outside_zero(second, 1)

    lam_b[...] = jnp.broadcast_to(column(liquid[...]), (species, parcels))
    sig_b[...] = jnp.broadcast_to(column(surface[...]), (species, parcels))
    gam_b[...] = jnp.broadcast_to(column(gasrate[...]), (species, cz))
    drop_in.wait()

    def droplet_block(b, carry):
        at = pl.ds(pl.multiple_of(b * 8, 8), 8)
        lam, sig = lam_b[at], sig_b[at]
        state = drop[:, at]
        unit = jnp.zeros((DROP_STEPS, 8, parcels), F32)
        base = jnp.zeros((8, parcels), F32)
        answer = jnp.zeros((8, parcels), F32)
        for _ in range(DROP_STEPS):
            flux = sig * state[-1]
            upper = jnp.concatenate([state[1:], state[-1:]], axis=0)
            lower = jnp.concatenate([state[1:2], state[:-1]], axis=0)
            state = state + lam[None] * (upper - 2.0 * state + lower)
            state = jnp.concatenate([state[:-1], (state[-1] - flux)[None]], axis=0)
            base = base + flux
            flux = sig * (unit[-1] - 1.0)
            upper = jnp.concatenate([unit[1:], unit[-1:]], axis=0)
            lower = jnp.concatenate([jnp.zeros_like(unit[:1]), unit[:-1]], axis=0)
            unit = unit + lam[None] * (upper - 2.0 * unit + lower)
            unit = jnp.concatenate([unit[:-1], (unit[-1] - flux)[None]], axis=0)
            answer = answer + flux
        drop[:, at] = state
        reply_b[:, at] = unit
        emit_b[0, at] = base
        emit_b[1, at] = answer
        return carry

    lax.fori_loop(0, species // 8, droplet_block, 0)
    place = lax.rem(rank, 4) * group + own
    chosen = (iota((half, parcels), 0) == place).astype(F32)
    low_half = rank < 4
    base = emit_b[0]
    base = jnp.concatenate([jnp.where(low_half, base, 0.0), jnp.where(low_half, 0.0, base)], axis=0)
    base_send[...] = exact_dot(chosen, base, NT).reshape(4, group, 2 * species)
    exchange(slab_row(base_send), slab_row(base_recv), base_ssem, base_rsem)

    await_all(meta_recv, meta_rsem)
    table = meta_recv[...]
    lane_slot = lax.rem(iota((group, 128), 1), 8)
    stacked = jnp.concatenate([jnp.where(lane_slot == j, table, 0.0) for j in range(8)], axis=0)
    gather_q = (iota((16, 128), 1) // 8 == iota((16, 128), 0)).astype(F32)
    byslot = exact_dot(gather_q, stacked, NT)
    ids = (byslot[0:STENCIL] + 0.5).astype(jnp.int32)
    vals = byslot[STENCIL:]
    total = vals
    for turn in range(1, STENCIL):
        same = pltpu.roll(ids, turn, 0) == ids
        total = total + jnp.where(same, pltpu.roll(vals, turn, 0), 0.0)
    sum_v = jnp.sum(vals, axis=0, keepdims=True)
    inv_mass = jnp.where(sum_v > 0.0, 1.0 / jnp.where(sum_v > 0.0, sum_v, 1.0), 0.0)
    r_f = (ids // cz).astype(F32)
    z_f = lax.rem(ids, cz).astype(F32)
    v_high = total.astype(BF16).astype(F32)
    v_low = total - v_high
    for h in range(2):
        for k in range(STENCIL):
            for ref, val in ((zk_s, z_f), (rk_s, r_f), (vh_s, v_high), (vl_s, v_low)):
                one = val[k:k + 1, h * half:(h + 1) * half]
                ref[h, k] = jnp.broadcast_to(one, (8, half))

    zero = jnp.zeros((16, half), BF16)

    def twice(value):
        return jnp.concatenate([value, value], axis=0).astype(BF16)

    def build(h, r, carry):
        at_row = jnp.full((8, half), r.astype(F32))
        key = [twice(jnp.where(rk_s[h, k] == at_row, zk_s[h, k], -1.0)) for k in range(STENCIL)]
        vh = [twice(vh_s[h, k]) for k in range(STENCIL)]
        vl = [twice(vl_s[h, k]) for k in range(STENCIL)]
        for chunk in range(cz // 16):
            z = (iota((16, half), 0) + chunk * 16).astype(F32).astype(BF16)
            high, low = zero, zero
            for k in reversed(range(STENCIL)):
                hit = key[k] == z
                high = jnp.where(hit, vh[k], high)
                low = jnp.where(hit, vl[k], low)
            w_hi[r, h, chunk * 16:chunk * 16 + 16] = high
            w_lo[r, h, chunk * 16:chunk * 16 + 16] = low
        return carry

    lax.fori_loop(0, rows, functools.partial(build, 0), 0)

    def merged(step):
        up = edge_recv[step, 1]
        down = edge_recv[step, 0]
        even = lax.rem(lane, 2) == 0
        return jnp.where(even, pltpu.roll(up, cz - 1, 1), pltpu.roll(down, 1, 1))

    def stencil(buf, halo, x, y):
        r = x * ny + y
        x, y = x + 1, y + 1
        mid = buf[x, y]
        beside = buf[x + 1, y] + buf[x - 1, y]
        beside = beside + buf[x, y + 1] + buf[x, y - 1]
        ends = pltpu.roll(halo, cz - 1 - 2 * r, 1)
        beside = beside + jnp.where(lane == cz - 1, ends, pltpu.roll(mid, cz - 1, 1))
        beside = beside + jnp.where(lane == 0, ends, pltpu.roll(mid, 1, 1))
        return mid + gam_b[...] * (beside - 6.0 * mid)

    await_faces(first, 0)
    halo = merged(0)

    def first_step(x, edges):
        for y in range(ny):
            field = stencil(first, halo, x, y)
            second[x + 1, y + 1] = field
            edges = edges + edge_part(field, x * ny + y)
        return edges

    edge_send[1] = lax.fori_loop(0, nx, first_step, jnp.zeros((species, cz), F32))
    start_faces(second, 1)

    lax.fori_loop(0, rows, functools.partial(build, 1), 0)

    acc_s[...] = jnp.zeros_like(acc_s)
    acc2_s[...] = jnp.zeros_like(acc2_s)

    def gather(g, carry):
        for h in range(2):
            at = slice(h * half, (h + 1) * half)
            one, two = acc_s[:, at], acc2_s[:, at]
            for k in range(4):
                i = 4 * g + k
                lhs = jnp.concatenate([parts[i, 0], parts[i, 1]], axis=1)
                hi = jnp.concatenate([w_hi[2 * i, h], w_hi[2 * i + 1, h]], axis=0)
                lo = jnp.concatenate([w_lo[2 * i, h], w_lo[2 * i + 1, h]], axis=0)
                one = one + dot(lhs, hi, NN)
                two = two + dot(lhs[0:species], lo, NN)
            acc_s[:, at] = one
            acc2_s[:, at] = two
        return carry

    lax.fori_loop(0, rows // 8, gather, 0)
    held = acc_s[0:species] + acc_s[species:] + acc2_s[...]
    gas_at = held * inv_mass
    back_send[...] = jnp.transpose(
        jnp.concatenate([gas_at[:, :half], gas_at[:, half:]], axis=0)
    ).reshape(4, group, 2 * species)
    exchange(slab_row(back_send), slab_row(back_recv), back_ssem, back_rsem)

    await_all(base_recv, base_rsem)
    got = jnp.transpose(base_recv[...].reshape(half, 2 * species))
    base = jnp.concatenate([got[0:species], got[species:]], axis=1)
    emitted = base + emit_b[1, :, 0:1] * gas_at
    high, low = split(emitted)
    both = jnp.concatenate([high, low], axis=0)

    await_faces(second, 1)
    halo2 = merged(1)

    def last_step(x, carry):
        for k in range(ny // 2):
            i = x * (ny // 2) + k
            hi = jnp.concatenate(
                [jnp.concatenate([w_hi[2 * i + t, 0], w_hi[2 * i + t, 1]], axis=1) for t in range(2)], axis=0
            )
            lo = jnp.concatenate(
                [jnp.concatenate([w_lo[2 * i + t, 0], w_lo[2 * i + t, 1]], axis=1) for t in range(2)], axis=0
            )
            one = dot(both, hi, NT)
            add = one[0:species] + one[species:] + dot(high, lo, NT)
            for t in range(2):
                field = stencil(second, halo2, x, 2 * k + t) + add[:, t * cz:(t + 1) * cz]
                out_s[pl.ds(2 * i + t, species, stride=rows), :] = field
        return carry

    lax.fori_loop(0, nx, last_step, 0)

    await_all(back_recv, back_rsem)
    got = jnp.transpose(back_recv[...].reshape(half, 2 * species))
    seen = exact_dot(got, chosen, NN)
    seen = jnp.where(low_half, seen[0:species], seen[species:])
    for i in range(DROP_STEPS):
        drop[nodes - DROP_STEPS + i] = drop[nodes - DROP_STEPS + i] + reply_b[i] * seen

    await_all(meta_send.at[most], meta_ssem)
    await_all(base_send.at[:, most], base_ssem)
    await_all(back_send.at[:, most], back_ssem)
    drain_faces(first, 0)
    drain_faces(second, 1)


def on_device(gas, droplet, owner, cells, weights, mass, liquid_rate, surface_rate, gas_rate):
    n_gx, n_gy, n_gz = (lax.axis_size(a) for a in ("gx", "gy", "gz"))
    species, nx, ny, cz = gas.shape
    nodes, _, parcels = droplet.shape
    group = n_gy * n_gz
    rows = nx * ny
    half = 4 * group
    vmem = pl.BlockSpec(memory_space=pltpu.VMEM)
    hbm = pl.BlockSpec(memory_space=pltpu.MemorySpace.HBM)
    dma = pltpu.SemaphoreType.DMA
    padded = pltpu.VMEM((nx + 2, ny + 2, species, cz), F32)
    slabs = pltpu.VMEM((4, group, 2 * species), F32)
    held = pltpu.VMEM((species, parcels), F32)
    onehot = pltpu.VMEM((rows, 2, cz, half), BF16)
    small = pltpu.VMEM((2, STENCIL, 8, half), F32)
    gas_next, droplet_next = pl.pallas_call(
        functools.partial(kernel, n_gx, n_gy, n_gz, nx, ny),
        out_shape=(
            jax.ShapeDtypeStruct((species * rows, cz), F32),
            jax.ShapeDtypeStruct(droplet.shape, F32),
        ),
        in_specs=[hbm] * 9,
        out_specs=(vmem, vmem),
        scratch_shapes=[
            pltpu.VMEM((1, parcels), jnp.int32), pltpu.VMEM((STENCIL, parcels), jnp.int32),
            pltpu.VMEM((STENCIL, parcels), F32), pltpu.VMEM((1, parcels), F32),
            pltpu.VMEM((1, species), F32), pltpu.VMEM((1, species), F32), pltpu.VMEM((1, species), F32),
            pltpu.VMEM((species * rows, cz), F32),
            padded, padded,
            pltpu.VMEM((rows // 2, 2, 2 * species, cz), BF16),
            held, held, pltpu.VMEM((species, cz), F32),
            pltpu.VMEM((DROP_STEPS, species, parcels), F32),
            pltpu.VMEM((2, species, parcels), F32),
            onehot, onehot, small, small, small, small,
            pltpu.VMEM((2 * species, 2 * half), F32),
            pltpu.VMEM((species, 2 * half), F32),
            pltpu.VMEM((group, 128), F32), pltpu.VMEM((group, 128), F32),
            slabs, slabs, slabs, slabs,
            pltpu.VMEM((2, species, cz), F32), pltpu.VMEM((2, 2, species, cz), F32),
            dma((2,)), dma((7,)),
            dma, dma, dma, dma, dma, dma,
            dma((2, 6)), dma((2, 6)),
        ],
        compiler_params=pltpu.CompilerParams(
            collective_id=0, has_side_effects=True, vmem_limit_bytes=40 << 20
        ),
        name="spray",
    )(*(
        pltpu.with_memory_space_constraint(a, pltpu.MemorySpace.HBM)
        for a in (
            gas.reshape(species * rows, cz), droplet, owner.reshape(1, parcels), cells, weights,
            mass.reshape(1, parcels), liquid_rate.reshape(1, species), surface_rate.reshape(1, species),
            gas_rate.reshape(1, species),
        )
    ))
    return gas_next.reshape(gas.shape), droplet_next


def solution(mesh):
    return jax.shard_map(
        on_device,
        mesh=mesh,
        in_specs=(
            P(None, "gx", "gy", "gz"),
            P(None, None, ("gx", "gy", "gz")),
            P(("gx", "gy", "gz"), None),
            P(None, ("gx", "gy", "gz")),
            P(None, ("gx", "gy", "gz")),
            P(("gx", "gy", "gz")),
            P(),
            P(),
            P(),
        ),
        out_specs=(P(None, "gx", "gy", "gz"), P(None, None, ("gx", "gy", "gz"))),
        check_vma=False,
    )
```

```python
import functools

import jax
import jax.numpy as jnp
from jax import lax
from jax.experimental import pallas as pl
from jax.experimental.pallas import tpu as pltpu
from jax.sharding import PartitionSpec as P

STENCIL = 8
DROP_STEPS = 4
MESH = pl.DeviceIdType.MESH
F32 = jnp.float32
BF16 = jnp.bfloat16
EXACT = lax.Precision.HIGHEST
NT = (((1,), (1,)), ((), ()))
NN = (((1,), (0,)), ((), ()))


def iota(shape, dim):
    return lax.broadcasted_iota(jnp.int32, shape, dim)


def column(row, lanes=None):
    n = row.shape[1]
    spread = jnp.broadcast_to(row, (n, n))
    picked = jnp.where(iota((n, n), 0) == iota((n, n), 1), spread, jnp.zeros_like(spread))
    return jnp.sum(picked, axis=1, keepdims=True)


def split(value):
    high = value.astype(BF16)
    low = (value - high.astype(F32)).astype(BF16)
    return high, low


def exact_dot(a, b, dims):
    return lax.dot_general(a, b, dims, precision=EXACT, preferred_element_type=F32)


def dot(a, b, dims):
    return lax.dot_general(a, b, dims, preferred_element_type=F32)


def kernel(
    n_gx, n_gy, n_gz, nx, ny,
    gas, droplet, owner_in, cells_in, weights_in, mass_in, liquid_in, surface_in, gasrate_in,
    out_s, drop,
    owner, cells, weights, mass, liquid, surface, gasrate,
    raw, first, second, parts, lam_b, sig_b, gam_b, reply_b, emit_b,
    w_hi, w_lo, zk_s, rk_s, vh_s, vl_s, acc_s, acc2_s,
    meta_send, meta_recv, base_send, base_recv, back_send, back_recv,
    edge_send, edge_recv,
    in_sem, small_sem,
    meta_ssem, meta_rsem, base_ssem, base_rsem, back_ssem, back_rsem,
    face_ssem, face_rsem,
):
    group = n_gy * n_gz
    rows = nx * ny
    half = 4 * group
    species = liquid.shape[1]
    nodes = droplet.shape[0]
    parcels = owner.shape[1]
    cz = 128

    gx = lax.axis_index("gx")
    gy = lax.axis_index("gy")
    gz = lax.axis_index("gz")
    me = gy * n_gz + gz

    shifted_z = [lax.rem(gz + b, n_gz) for b in range(n_gz)]

    def each_peer(act):
        def turn(a, carry):
            to_y = lax.rem(gy + a, n_gy)
            for b in range(n_gz):
                to_z = shifted_z[b]
                run = functools.partial(act, to_y * n_gz + to_z, {"gy": to_y, "gz": to_z})
                if b == 0:
                    pl.when(a > 0)(run)
                else:
                    run()
            return carry

        lax.fori_loop(0, n_gy, turn, 0)

    smalls = [
        pltpu.make_async_copy(src, dst, small_sem.at[i])
        for i, (src, dst) in enumerate((
            (owner_in, owner), (cells_in, cells), (weights_in, weights), (mass_in, mass),
            (liquid_in, liquid), (surface_in, surface), (gasrate_in, gasrate),
        ))
    ]
    for copy in smalls:
        copy.start()
    gas_in = pltpu.make_async_copy(gas, raw, in_sem.at[0])
    gas_in.start()
    drop_in = pltpu.make_async_copy(droplet, drop, in_sem.at[1])
    drop_in.start()

    barrier = pltpu.get_barrier_semaphore()

    each_peer(lambda o, where: pl.semaphore_signal(
        barrier, inc=1, device_id=where, device_id_type=MESH
    ))
    for step in (1, n_gx - 1):
        pl.semaphore_signal(
            barrier, inc=1, device_id={"gx": lax.rem(gx + step, n_gx)}, device_id_type=MESH
        )

    for copy in smalls:
        copy.wait()
    own = owner[...]
    own_col = column(own)
    before = (own_col == own) & (iota((parcels, parcels), 0) < iota((parcels, parcels), 1))
    rank = jnp.sum(before.astype(F32), axis=0, keepdims=True).astype(jnp.int32)
    onehot = (iota((group, parcels), 0) == own).astype(F32)
    slot = (iota((8, parcels), 0) == rank).astype(F32)
    wts = weights[...]
    wts = wts / jnp.sum(wts, axis=0, keepdims=True)
    wts = wts * mass[...]
    cell = cells[...]
    cell_f = cell.astype(F32)
    tiles = [cell_f[q:q + 1] * slot for q in range(STENCIL)]
    tiles += [wts[q:q + 1] * slot for q in range(STENCIL)]
    spread = jnp.concatenate(tiles, axis=0)
    meta_send[...] = exact_dot(onehot, spread, NT)

    pl.semaphore_wait(barrier, group + 1)

    def exchange(src_of, dst_of, ssem, rsem):
        each_peer(lambda o, where: pltpu.make_async_remote_copy(
            src_ref=src_of(o), dst_ref=dst_of(me), send_sem=ssem, recv_sem=rsem,
            device_id=where, device_id_type=MESH,
        ).start())
        pltpu.make_async_copy(src_of(me), dst_of(me), rsem).start()

    def await_all(ref, sem):
        pltpu.make_async_copy(ref, ref, sem).wait()

    most = pl.ds(0, group - 1)

    meta_row = lambda ref: (lambda o: ref.at[pl.ds(o, 1)])
    slab_row = lambda ref: (lambda o: ref.at[:, pl.ds(o, 1)])

    exchange(meta_row(meta_send), meta_row(meta_recv), meta_ssem, meta_rsem)

    def faces(buf, step):
        inner_x, inner_y = pl.ds(1, nx), pl.ds(1, ny)
        table = [
            (gx > 0, {"gx": gx - 1}, buf.at[1, inner_y], buf.at[nx + 1, inner_y], gx < n_gx - 1),
            (gx < n_gx - 1, {"gx": gx + 1}, buf.at[nx, inner_y], buf.at[0, inner_y], gx > 0),
            (gy > 0, {"gy": gy - 1}, buf.at[inner_x, 1], buf.at[inner_x, ny + 1], gy < n_gy - 1),
            (gy < n_gy - 1, {"gy": gy + 1}, buf.at[inner_x, ny], buf.at[inner_x, 0], gy > 0),
            (gz > 0, {"gz": gz - 1}, edge_send.at[step], edge_recv.at[step, 1], gz < n_gz - 1),
            (gz < n_gz - 1, {"gz": gz + 1}, edge_send.at[step], edge_recv.at[step, 0], gz > 0),
        ]
        out = []
        for i, (send_if, target, src, dst, recv_if) in enumerate(table):
            copy = pltpu.make_async_remote_copy(
                src_ref=src, dst_ref=dst, send_sem=face_ssem.at[step, i],
                recv_sem=face_rsem.at[step, i], device_id=target, device_id_type=MESH,
            )
            out.append((send_if, copy, recv_if, dst))
        return out

    def start_faces(buf, step):
        for send_if, copy, _, _ in faces(buf, step):
            pl.when(send_if)(copy.start)

    def await_faces(buf, step):
        for i, (_, _, recv_if, dst) in enumerate(faces(buf, step)):
            wait = pltpu.make_async_copy(dst, dst, face_rsem.at[step, i]).wait
            pl.when(recv_if)(wait)

    def drain_faces(buf, step):
        for send_if, copy, _, _ in faces(buf, step):
            pl.when(send_if)(copy.wait_send)

    def outside_zero(buf, step):
        zero_x = jnp.zeros((ny, species, cz), F32)
        zero_y = jnp.zeros((nx, species, cz), F32)
        zero_z = jnp.zeros((species, cz), F32)

        @pl.when(gx == 0)
        def _():
            buf[0, 1:ny + 1] = zero_x

        @pl.when(gx == n_gx - 1)
        def _():
            buf[nx + 1, 1:ny + 1] = zero_x

        @pl.when(gy == 0)
        def _():
            buf[1:nx + 1, 0] = zero_y

        @pl.when(gy == n_gy - 1)
        def _():
            buf[1:nx + 1, ny + 1] = zero_y

        @pl.when(gz == 0)
        def _():
            edge_recv[step, 0] = zero_z

        @pl.when(gz == n_gz - 1)
        def _():
            edge_recv[step, 1] = zero_z

    lane = iota((species, cz), 1)
    def edge_part(field, r):
        return jnp.where(lane // 2 == r, pltpu.roll(field, 2 * r + 1, 1), 0.0)

    gas_in.wait()

    def load_rows(x, edges):
        for y in range(ny):
            r = x * ny + y
            field = raw[pl.ds(r, species, stride=rows), :]
            first[x + 1, y + 1] = field
            high, low = split(field)
            pair = x * (ny // 2) + y // 2
            parts[pair, y % 2, 0:species] = high
            parts[pair, y % 2, species:2 * species] = low
            edges = edges + edge_part(field, r)
        return edges

    edge_send[0] = lax.fori_loop(0, nx, load_rows, jnp.zeros((species, cz), F32))
    start_faces(first, 0)
    outside_zero(first, 0)
    outside_zero(second, 1)

    lam_b[...] = jnp.broadcast_to(column(liquid[...]), (species, parcels))
    sig_b[...] = jnp.broadcast_to(column(surface[...]), (species, parcels))
    gam_b[...] = jnp.broadcast_to(column(gasrate[...]), (species, cz))
    drop_in.wait()

    def droplet_block(b, carry):
        at = pl.ds(pl.multiple_of(b * 8, 8), 8)
        lam, sig = lam_b[at], sig_b[at]
        state = drop[:, at]
        unit = jnp.zeros((DROP_STEPS, 8, parcels), F32)
        base = jnp.zeros((8, parcels), F32)
        answer = jnp.zeros((8, parcels), F32)
        for _ in range(DROP_STEPS):
            flux = sig * state[-1]
            upper = jnp.concatenate([state[1:], state[-1:]], axis=0)
            lower = jnp.concatenate([state[1:2], state[:-1]], axis=0)
            state = state + lam[None] * (upper - 2.0 * state + lower)
            state = jnp.concatenate([state[:-1], (state[-1] - flux)[None]], axis=0)
            base = base + flux
            flux = sig * (unit[-1] - 1.0)
            upper = jnp.concatenate([unit[1:], unit[-1:]], axis=0)
            lower = jnp.concatenate([jnp.zeros_like(unit[:1]), unit[:-1]], axis=0)
            unit = unit + lam[None] * (upper - 2.0 * unit + lower)
            unit = jnp.concatenate([unit[:-1], (unit[-1] - flux)[None]], axis=0)
            answer = answer + flux
        drop[:, at] = state
        reply_b[:, at] = unit
        emit_b[0, at] = base
        emit_b[1, at] = answer
        return carry

    lax.fori_loop(0, species // 8, droplet_block, 0)
    place = lax.rem(rank, 4) * group + own
    chosen = (iota((half, parcels), 0) == place).astype(F32)
    low_half = rank < 4
    base = emit_b[0]
    base = jnp.concatenate([jnp.where(low_half, base, 0.0), jnp.where(low_half, 0.0, base)], axis=0)
    base_send[...] = exact_dot(chosen, base, NT).reshape(4, group, 2 * species)
    exchange(slab_row(base_send), slab_row(base_recv), base_ssem, base_rsem)

    await_all(meta_recv, meta_rsem)
    table = meta_recv[...]
    lane_slot = lax.rem(iota((group, 128), 1), 8)
    stacked = jnp.concatenate([jnp.where(lane_slot == j, table, 0.0) for j in range(8)], axis=0)
    gather_q = (iota((16, 128), 1) // 8 == iota((16, 128), 0)).astype(F32)
    byslot = exact_dot(gather_q, stacked, NT)
    ids = (byslot[0:STENCIL] + 0.5).astype(jnp.int32)
    vals = byslot[STENCIL:]
    total = vals
    for turn in range(1, STENCIL):
        same = pltpu.roll(ids, turn, 0) == ids
        total = total + jnp.where(same, pltpu.roll(vals, turn, 0), 0.0)
    sum_v = jnp.sum(vals, axis=0, keepdims=True)
    inv_mass = jnp.where(sum_v > 0.0, 1.0 / jnp.where(sum_v > 0.0, sum_v, 1.0), 0.0)
    r_f = (ids // cz).astype(F32)
    z_f = lax.rem(ids, cz).astype(F32)
    v_high = total.astype(BF16).astype(F32)
    v_low = total - v_high
    for h in range(2):
        for k in range(STENCIL):
            for ref, val in ((zk_s, z_f), (rk_s, r_f), (vh_s, v_high), (vl_s, v_low)):
                one = val[k:k + 1, h * half:(h + 1) * half]
                ref[h, k] = jnp.broadcast_to(one, (8, half))

    zero = jnp.zeros((16, half), BF16)

    def twice(value):
        return jnp.concatenate([value, value], axis=0).astype(BF16)

    def build(h, r):
        at_row = jnp.full((8, half), jnp.asarray(r).astype(F32))
        key = [twice(jnp.where(rk_s[h, k] == at_row, zk_s[h, k], -1.0)) for k in range(STENCIL)]
        vh = [twice(vh_s[h, k]) for k in range(STENCIL)]
        vl = [twice(vl_s[h, k]) for k in range(STENCIL)]
        for chunk in range(cz // 16):
            z = (iota((16, half), 0) + chunk * 16).astype(F32).astype(BF16)
            high, low = zero, zero
            for k in reversed(range(STENCIL)):
                hit = key[k] == z
                high = jnp.where(hit, vh[k], high)
                low = jnp.where(hit, vl[k], low)
            w_hi[r, h, chunk * 16:chunk * 16 + 16] = high
            w_lo[r, h, chunk * 16:chunk * 16 + 16] = low

    def product(h, i):
        at = slice(h * half, (h + 1) * half)
        lhs = jnp.concatenate([parts[i, 0], parts[i, 1]], axis=1)
        hi = jnp.concatenate([w_hi[2 * i, h], w_hi[2 * i + 1, h]], axis=0)
        lo = jnp.concatenate([w_lo[2 * i, h], w_lo[2 * i + 1, h]], axis=0)
        acc_s[:, at] += dot(lhs, hi, NN)
        acc2_s[:, at] += dot(lhs[0:species], lo, NN)

    def gather_half(h):
        build(h, 0)
        build(h, 1)

        def pair(i, carry):
            product(h, i - 1)
            build(h, 2 * i)
            build(h, 2 * i + 1)
            return carry

        lax.fori_loop(1, rows // 2, pair, 0)
        product(h, rows // 2 - 1)

    acc_s[...] = jnp.zeros_like(acc_s)
    acc2_s[...] = jnp.zeros_like(acc2_s)

    gather_half(0)

    def merged(step):
        up = edge_recv[step, 1]
        down = edge_recv[step, 0]
        even = lax.rem(lane, 2) == 0
        return jnp.where(even, pltpu.roll(up, cz - 1, 1), pltpu.roll(down, 1, 1))

    def stencil(buf, halo, x, y):
        r = x * ny + y
        x, y = x + 1, y + 1
        mid = buf[x, y]
        beside = buf[x + 1, y] + buf[x - 1, y]
        beside = beside + buf[x, y + 1] + buf[x, y - 1]
        ends = pltpu.roll(halo, cz - 1 - 2 * r, 1)
        beside = beside + jnp.where(lane == cz - 1, ends, pltpu.roll(mid, cz - 1, 1))
        beside = beside + jnp.where(lane == 0, ends, pltpu.roll(mid, 1, 1))
        return mid + gam_b[...] * (beside - 6.0 * mid)

    await_faces(first, 0)
    halo = merged(0)

    def first_step(x, edges):
        for y in range(ny):
            field = stencil(first, halo, x, y)
            second[x + 1, y + 1] = field
            edges = edges + edge_part(field, x * ny + y)
        return edges

    edge_send[1] = lax.fori_loop(0, nx, first_step, jnp.zeros((species, cz), F32))
    start_faces(second, 1)

    gather_half(1)
    held = acc_s[0:species] + acc_s[species:] + acc2_s[...]
    gas_at = held * inv_mass
    back_send[...] = jnp.transpose(
        jnp.concatenate([gas_at[:, :half], gas_at[:, half:]], axis=0)
    ).reshape(4, group, 2 * species)
    exchange(slab_row(back_send), slab_row(back_recv), back_ssem, back_rsem)

    await_all(base_recv, base_rsem)
    got = jnp.transpose(base_recv[...].reshape(half, 2 * species))
    base = jnp.concatenate([got[0:species], got[species:]], axis=1)
    emitted = base + emit_b[1, :, 0:1] * gas_at
    high, low = split(emitted)
    both = jnp.concatenate([high, low], axis=0)

    await_faces(second, 1)
    halo2 = merged(1)

    def last_step(x, carry):
        for k in range(ny // 2):
            i = x * (ny // 2) + k
            hi = jnp.concatenate(
                [jnp.concatenate([w_hi[2 * i + t, 0], w_hi[2 * i + t, 1]], axis=1) for t in range(2)], axis=0
            )
            lo = jnp.concatenate(
                [jnp.concatenate([w_lo[2 * i + t, 0], w_lo[2 * i + t, 1]], axis=1) for t in range(2)], axis=0
            )
            one = dot(both, hi, NT)
            add = one[0:species] + one[species:] + dot(high, lo, NT)
            for t in range(2):
                field = stencil(second, halo2, x, 2 * k + t) + add[:, t * cz:(t + 1) * cz]
                out_s[pl.ds(2 * i + t, species, stride=rows), :] = field
        return carry

    lax.fori_loop(0, nx, last_step, 0)

    await_all(back_recv, back_rsem)
    got = jnp.transpose(back_recv[...].reshape(half, 2 * species))
    seen = exact_dot(got, chosen, NN)
    seen = jnp.where(low_half, seen[0:species], seen[species:])
    for i in range(DROP_STEPS):
        drop[nodes - DROP_STEPS + i] = drop[nodes - DROP_STEPS + i] + reply_b[i] * seen

    await_all(meta_send.at[most], meta_ssem)
    await_all(base_send.at[:, most], base_ssem)
    await_all(back_send.at[:, most], back_ssem)
    drain_faces(first, 0)
    drain_faces(second, 1)


def store(gas, droplet, gas_out, drop_out, sem):
    copies = []
    for i, (src, dst) in enumerate(((gas, gas_out), (droplet, drop_out))):
        step = src.shape[0] // 4
        for k in range(4):
            at = pl.ds(k * step, step)
            copies.append(pltpu.make_async_copy(src.at[at], dst.at[at], sem.at[i, k]))
    for copy in copies:
        copy.start()
    for copy in copies:
        copy.wait()


def on_device(gas, droplet, owner, cells, weights, mass, liquid_rate, surface_rate, gas_rate):
    n_gx, n_gy, n_gz = (lax.axis_size(a) for a in ("gx", "gy", "gz"))
    species, nx, ny, cz = gas.shape
    nodes, _, parcels = droplet.shape
    group = n_gy * n_gz
    rows = nx * ny
    half = 4 * group
    vmem = pl.BlockSpec(memory_space=pltpu.VMEM)
    hbm = pl.BlockSpec(memory_space=pltpu.MemorySpace.HBM)
    dma = pltpu.SemaphoreType.DMA
    padded = pltpu.VMEM((nx + 2, ny + 2, species, cz), F32)
    slabs = pltpu.VMEM((4, group, 2 * species), F32)
    held = pltpu.VMEM((species, parcels), F32)
    onehot = pltpu.VMEM((rows, 2, cz, half), BF16)
    small = pltpu.VMEM((2, STENCIL, 8, half), F32)
    gas_next, droplet_next = pl.pallas_call(
        functools.partial(kernel, n_gx, n_gy, n_gz, nx, ny),
        out_shape=(
            jax.ShapeDtypeStruct((species * rows, cz), F32),
            jax.ShapeDtypeStruct(droplet.shape, F32),
        ),
        in_specs=[hbm] * 9,
        out_specs=(vmem, vmem),
        scratch_shapes=[
            pltpu.VMEM((1, parcels), jnp.int32), pltpu.VMEM((STENCIL, parcels), jnp.int32),
            pltpu.VMEM((STENCIL, parcels), F32), pltpu.VMEM((1, parcels), F32),
            pltpu.VMEM((1, species), F32), pltpu.VMEM((1, species), F32), pltpu.VMEM((1, species), F32),
            pltpu.VMEM((species * rows, cz), F32),
            padded, padded,
            pltpu.VMEM((rows // 2, 2, 2 * species, cz), BF16),
            held, held, pltpu.VMEM((species, cz), F32),
            pltpu.VMEM((DROP_STEPS, species, parcels), F32),
            pltpu.VMEM((2, species, parcels), F32),
            onehot, onehot, small, small, small, small,
            pltpu.VMEM((2 * species, 2 * half), F32),
            pltpu.VMEM((species, 2 * half), F32),
            pltpu.VMEM((group, 128), F32), pltpu.VMEM((group, 128), F32),
            slabs, slabs, slabs, slabs,
            pltpu.VMEM((2, species, cz), F32), pltpu.VMEM((2, 2, species, cz), F32),
            dma((2,)), dma((7,)),
            dma, dma, dma, dma, dma, dma,
            dma((2, 6)), dma((2, 6)),
        ],
        compiler_params=pltpu.CompilerParams(
            collective_id=0, has_side_effects=True, vmem_limit_bytes=40 << 20
        ),
        name="spray",
    )(*(
        pltpu.with_memory_space_constraint(a, pltpu.MemorySpace.HBM)
        for a in (
            gas.reshape(species * rows, cz), droplet, owner.reshape(1, parcels), cells, weights,
            mass.reshape(1, parcels), liquid_rate.reshape(1, species), surface_rate.reshape(1, species),
            gas_rate.reshape(1, species),
        )
    ))
    gas_next, droplet_next = pl.pallas_call(
        store,
        out_shape=(
            jax.ShapeDtypeStruct((species * rows, cz), F32),
            jax.ShapeDtypeStruct(droplet.shape, F32),
        ),
        in_specs=[vmem, vmem],
        out_specs=(hbm, hbm),
        scratch_shapes=[dma((2, 4))],
        name="store",
    )(*(
        pltpu.with_memory_space_constraint(a, pltpu.MemorySpace.VMEM) for a in (gas_next, droplet_next)
    ))
    return gas_next.reshape(gas.shape), droplet_next


def solution(mesh):
    return jax.shard_map(
        on_device,
        mesh=mesh,
        in_specs=(
            P(None, "gx", "gy", "gz"),
            P(None, None, ("gx", "gy", "gz")),
            P(("gx", "gy", "gz"), None),
            P(None, ("gx", "gy", "gz")),
            P(None, ("gx", "gy", "gz")),
            P(("gx", "gy", "gz")),
            P(),
            P(),
            P(),
        ),
        out_specs=(P(None, "gx", "gy", "gz"), P(None, None, ("gx", "gy", "gz"))),
        check_vma=False,
    )
```

```python
import functools

import jax
import jax.numpy as jnp
from jax import lax
from jax.experimental import pallas as pl
from jax.experimental.pallas import tpu as pltpu
from jax.sharding import PartitionSpec as P

STENCIL = 8
DROP_STEPS = 4
MESH = pl.DeviceIdType.MESH
F32 = jnp.float32
BF16 = jnp.bfloat16
EXACT = lax.Precision.HIGHEST
NT = (((1,), (1,)), ((), ()))
NN = (((1,), (0,)), ((), ()))


def iota(shape, dim):
    return lax.broadcasted_iota(jnp.int32, shape, dim)


def column(row, lanes=None):
    n = row.shape[1]
    spread = jnp.broadcast_to(row, (n, n))
    picked = jnp.where(iota((n, n), 0) == iota((n, n), 1), spread, jnp.zeros_like(spread))
    return jnp.sum(picked, axis=1, keepdims=True)


def split(value):
    high = value.astype(BF16)
    low = (value - high.astype(F32)).astype(BF16)
    return high, low


def exact_dot(a, b, dims):
    return lax.dot_general(a, b, dims, precision=EXACT, preferred_element_type=F32)


def dot(a, b, dims):
    return lax.dot_general(a, b, dims, preferred_element_type=F32)


def kernel(
    n_gx, n_gy, n_gz, nx, ny,
    gas, droplet, owner_in, cells_in, weights_in, mass_in, liquid_in, surface_in, gasrate_in,
    out_s, drop,
    owner, cells, weights, mass, liquid, surface, gasrate,
    raw, first, second, parts, lam_b, sig_b, gam_b, reply_b, emit_b,
    w_hi, w_lo, zk_s, rk_s, vh_s, vl_s, acc_s, acc2_s,
    meta_send, meta_recv, base_send, base_recv, back_send, back_recv,
    edge_send, edge_recv,
    in_sem, small_sem,
    meta_ssem, meta_rsem, base_ssem, base_rsem, back_ssem, back_rsem,
    face_ssem, face_rsem,
):
    group = n_gy * n_gz
    rows = nx * ny
    half = 4 * group
    species = liquid.shape[1]
    nodes = droplet.shape[0]
    parcels = owner.shape[1]
    cz = 128

    gx = lax.axis_index("gx")
    gy = lax.axis_index("gy")
    gz = lax.axis_index("gz")
    me = gy * n_gz + gz

    shifted_z = [lax.rem(gz + b, n_gz) for b in range(n_gz)]

    def each_peer(act):
        def turn(a, carry):
            to_y = lax.rem(gy + a, n_gy)
            for b in range(n_gz):
                to_z = shifted_z[b]
                run = functools.partial(act, to_y * n_gz + to_z, {"gy": to_y, "gz": to_z})
                if b == 0:
                    pl.when(a > 0)(run)
                else:
                    run()
            return carry

        lax.fori_loop(0, n_gy, turn, 0)

    smalls = [
        pltpu.make_async_copy(src, dst, small_sem.at[i])
        for i, (src, dst) in enumerate((
            (owner_in, owner), (cells_in, cells), (weights_in, weights), (mass_in, mass),
            (liquid_in, liquid), (surface_in, surface), (gasrate_in, gasrate),
        ))
    ]
    for copy in smalls:
        copy.start()
    gas_in = pltpu.make_async_copy(gas, raw, in_sem.at[0])
    gas_in.start()
    drop_in = pltpu.make_async_copy(droplet, drop, in_sem.at[1])
    drop_in.start()

    barrier = pltpu.get_barrier_semaphore()

    each_peer(lambda o, where: pl.semaphore_signal(
        barrier, inc=1, device_id=where, device_id_type=MESH
    ))
    for step in (1, n_gx - 1):
        pl.semaphore_signal(
            barrier, inc=1, device_id={"gx": lax.rem(gx + step, n_gx)}, device_id_type=MESH
        )

    for copy in smalls:
        copy.wait()
    own = owner[...]
    own_col = column(own)
    before = (own_col == own) & (iota((parcels, parcels), 0) < iota((parcels, parcels), 1))
    rank = jnp.sum(before.astype(F32), axis=0, keepdims=True).astype(jnp.int32)
    onehot = (iota((group, parcels), 0) == own).astype(F32)
    slot = (iota((8, parcels), 0) == rank).astype(F32)
    wts = weights[...]
    wts = wts / jnp.sum(wts, axis=0, keepdims=True)
    wts = wts * mass[...]
    cell = cells[...]
    cell_f = cell.astype(F32)
    tiles = [cell_f[q:q + 1] * slot for q in range(STENCIL)]
    tiles += [wts[q:q + 1] * slot for q in range(STENCIL)]
    spread = jnp.concatenate(tiles, axis=0)
    meta_send[...] = exact_dot(onehot, spread, NT)

    pl.semaphore_wait(barrier, group + 1)

    def exchange(src_of, dst_of, ssem, rsem):
        each_peer(lambda o, where: pltpu.make_async_remote_copy(
            src_ref=src_of(o), dst_ref=dst_of(me), send_sem=ssem, recv_sem=rsem,
            device_id=where, device_id_type=MESH,
        ).start())
        pltpu.make_async_copy(src_of(me), dst_of(me), rsem).start()

    def await_all(ref, sem):
        pltpu.make_async_copy(ref, ref, sem).wait()

    most = pl.ds(0, group - 1)

    meta_row = lambda ref: (lambda o: ref.at[pl.ds(o, 1)])
    slab_row = lambda ref: (lambda o: ref.at[:, pl.ds(o, 1)])

    exchange(meta_row(meta_send), meta_row(meta_recv), meta_ssem, meta_rsem)

    def faces(buf, step):
        inner_x, inner_y = pl.ds(1, nx), pl.ds(1, ny)
        table = [
            (gx > 0, {"gx": gx - 1}, buf.at[1, inner_y], buf.at[nx + 1, inner_y], gx < n_gx - 1),
            (gx < n_gx - 1, {"gx": gx + 1}, buf.at[nx, inner_y], buf.at[0, inner_y], gx > 0),
            (gy > 0, {"gy": gy - 1}, buf.at[inner_x, 1], buf.at[inner_x, ny + 1], gy < n_gy - 1),
            (gy < n_gy - 1, {"gy": gy + 1}, buf.at[inner_x, ny], buf.at[inner_x, 0], gy > 0),
            (gz > 0, {"gz": gz - 1}, edge_send.at[step], edge_recv.at[step, 1], gz < n_gz - 1),
            (gz < n_gz - 1, {"gz": gz + 1}, edge_send.at[step], edge_recv.at[step, 0], gz > 0),
        ]
        out = []
        for i, (send_if, target, src, dst, recv_if) in enumerate(table):
            copy = pltpu.make_async_remote_copy(
                src_ref=src, dst_ref=dst, send_sem=face_ssem.at[step, i],
                recv_sem=face_rsem.at[step, i], device_id=target, device_id_type=MESH,
            )
            out.append((send_if, copy, recv_if, dst))
        return out

    def start_faces(buf, step):
        for send_if, copy, _, _ in faces(buf, step):
            pl.when(send_if)(copy.start)

    def await_faces(buf, step):
        for i, (_, _, recv_if, dst) in enumerate(faces(buf, step)):
            wait = pltpu.make_async_copy(dst, dst, face_rsem.at[step, i]).wait
            pl.when(recv_if)(wait)

    def drain_faces(buf, step):
        for send_if, copy, _, _ in faces(buf, step):
            pl.when(send_if)(copy.wait_send)

    def outside_zero(buf, step):
        zero_x = jnp.zeros((ny, species, cz), F32)
        zero_y = jnp.zeros((nx, species, cz), F32)
        zero_z = jnp.zeros((species, cz), F32)

        @pl.when(gx == 0)
        def _():
            buf[0, 1:ny + 1] = zero_x

        @pl.when(gx == n_gx - 1)
        def _():
            buf[nx + 1, 1:ny + 1] = zero_x

        @pl.when(gy == 0)
        def _():
            buf[1:nx + 1, 0] = zero_y

        @pl.when(gy == n_gy - 1)
        def _():
            buf[1:nx + 1, ny + 1] = zero_y

        @pl.when(gz == 0)
        def _():
            edge_recv[step, 0] = zero_z

        @pl.when(gz == n_gz - 1)
        def _():
            edge_recv[step, 1] = zero_z

    lane = iota((species, cz), 1)
    def edge_part(field, r):
        return jnp.where(lane // 2 == r, pltpu.roll(field, 2 * r + 1, 1), 0.0)

    gas_in.wait()

    def load_rows(x, edges):
        for y in range(ny):
            r = x * ny + y
            field = raw[pl.ds(r, species, stride=rows), :]
            first[x + 1, y + 1] = field
            high, low = split(field)
            pair = x * (ny // 2) + y // 2
            parts[pair, y % 2, 0:species] = high
            parts[pair, y % 2, species:2 * species] = low
            edges = edges + edge_part(field, r)
        return edges

    edge_send[0] = lax.fori_loop(0, nx, load_rows, jnp.zeros((species, cz), F32))
    start_faces(first, 0)
    outside_zero(first, 0)
    outside_zero(second, 1)

    lam_b[...] = jnp.broadcast_to(column(liquid[...]), (species, parcels))
    sig_b[...] = jnp.broadcast_to(column(surface[...]), (species, parcels))
    gam_b[...] = jnp.broadcast_to(column(gasrate[...]), (species, cz))
    drop_in.wait()

    def droplet_block(b, carry):
        at = pl.ds(pl.multiple_of(b * 8, 8), 8)
        lam, sig = lam_b[at], sig_b[at]
        state = drop[:, at]
        unit = jnp.zeros((DROP_STEPS, 8, parcels), F32)
        base = jnp.zeros((8, parcels), F32)
        answer = jnp.zeros((8, parcels), F32)
        for _ in range(DROP_STEPS):
            flux = sig * state[-1]
            upper = jnp.concatenate([state[1:], state[-1:]], axis=0)
            lower = jnp.concatenate([state[1:2], state[:-1]], axis=0)
            state = state + lam[None] * (upper - 2.0 * state + lower)
            state = jnp.concatenate([state[:-1], (state[-1] - flux)[None]], axis=0)
            base = base + flux
            flux = sig * (unit[-1] - 1.0)
            upper = jnp.concatenate([unit[1:], unit[-1:]], axis=0)
            lower = jnp.concatenate([jnp.zeros_like(unit[:1]), unit[:-1]], axis=0)
            unit = unit + lam[None] * (upper - 2.0 * unit + lower)
            unit = jnp.concatenate([unit[:-1], (unit[-1] - flux)[None]], axis=0)
            answer = answer + flux
        drop[:, at] = state
        reply_b[:, at] = unit
        emit_b[0, at] = base
        emit_b[1, at] = answer
        return carry

    lax.fori_loop(0, species // 8, droplet_block, 0)
    place = lax.rem(rank, 4) * group + own
    chosen = (iota((half, parcels), 0) == place).astype(F32)
    low_half = rank < 4
    base = emit_b[0]
    base = jnp.concatenate([jnp.where(low_half, base, 0.0), jnp.where(low_half, 0.0, base)], axis=0)
    base_send[...] = exact_dot(chosen, base, NT).reshape(4, group, 2 * species)
    exchange(slab_row(base_send), slab_row(base_recv), base_ssem, base_rsem)

    await_all(meta_recv, meta_rsem)
    table = meta_recv[...]
    lane_slot = lax.rem(iota((group, 128), 1), 8)
    stacked = jnp.concatenate([jnp.where(lane_slot == j, table, 0.0) for j in range(8)], axis=0)
    gather_q = (iota((16, 128), 1) // 8 == iota((16, 128), 0)).astype(F32)
    byslot = exact_dot(gather_q, stacked, NT)
    ids = (byslot[0:STENCIL] + 0.5).astype(jnp.int32)
    vals = byslot[STENCIL:]
    total = vals
    for turn in range(1, STENCIL):
        same = pltpu.roll(ids, turn, 0) == ids
        total = total + jnp.where(same, pltpu.roll(vals, turn, 0), 0.0)
    sum_v = jnp.sum(vals, axis=0, keepdims=True)
    inv_mass = jnp.where(sum_v > 0.0, 1.0 / jnp.where(sum_v > 0.0, sum_v, 1.0), 0.0)
    r_f = (ids // cz).astype(F32)
    z_f = lax.rem(ids, cz).astype(F32)
    v_high = total.astype(BF16).astype(F32)
    v_low = total - v_high
    for h in range(2):
        for k in range(STENCIL):
            for ref, val in ((zk_s, z_f), (rk_s, r_f), (vh_s, v_high), (vl_s, v_low)):
                one = val[k:k + 1, h * half:(h + 1) * half]
                ref[h, k] = jnp.broadcast_to(one, (8, half))

    zero = jnp.zeros((16, half), BF16)

    def twice(value):
        return jnp.concatenate([value, value], axis=0).astype(BF16)

    def build_row(h, r):
        at_row = jnp.full((8, half), r.astype(F32))
        key = [twice(jnp.where(rk_s[h, k] == at_row, zk_s[h, k], -1.0)) for k in range(STENCIL)]
        vh = [twice(vh_s[h, k]) for k in range(STENCIL)]
        vl = [twice(vl_s[h, k]) for k in range(STENCIL)]
        for chunk in range(cz // 16):
            z = (iota((16, half), 0) + chunk * 16).astype(F32).astype(BF16)
            high, low = zero, zero
            for k in reversed(range(STENCIL)):
                hit = key[k] == z
                high = jnp.where(hit, vh[k], high)
                low = jnp.where(hit, vl[k], low)
            w_hi[r, h, chunk * 16:chunk * 16 + 16] = high
            w_lo[r, h, chunk * 16:chunk * 16 + 16] = low

    def build(h, i, carry):
        build_row(h, 2 * i)
        build_row(h, 2 * i + 1)
        return carry

    def merged(step):
        up = edge_recv[step, 1]
        down = edge_recv[step, 0]
        even = lax.rem(lane, 2) == 0
        return jnp.where(even, pltpu.roll(up, cz - 1, 1), pltpu.roll(down, 1, 1))

    def stencil(buf, halo, x, y):
        r = x * ny + y
        x, y = x + 1, y + 1
        mid = buf[x, y]
        beside = buf[x + 1, y] + buf[x - 1, y]
        beside = beside + buf[x, y + 1] + buf[x, y - 1]
        ends = pltpu.roll(halo, cz - 1 - 2 * r, 1)
        beside = beside + jnp.where(lane == cz - 1, ends, pltpu.roll(mid, cz - 1, 1))
        beside = beside + jnp.where(lane == 0, ends, pltpu.roll(mid, 1, 1))
        return mid + gam_b[...] * (beside - 6.0 * mid)

    await_faces(first, 0)
    halo = merged(0)

    def first_step(x, edges):
        for y in range(ny):
            field = stencil(first, halo, x, y)
            second[x + 1, y + 1] = field
            edges = edges + edge_part(field, x * ny + y)
        return edges

    edge_send[1] = lax.fori_loop(0, nx, first_step, jnp.zeros((species, cz), F32))
    start_faces(second, 1)
    lax.fori_loop(0, rows // 2, functools.partial(build, 0), 0)


    lax.fori_loop(0, rows // 2, functools.partial(build, 1), 0)

    acc_s[...] = jnp.zeros_like(acc_s)
    acc2_s[...] = jnp.zeros_like(acc2_s)

    def gather(g, carry):
        for h in range(2):
            at = slice(h * half, (h + 1) * half)
            one, two = acc_s[:, at], acc2_s[:, at]
            for k in range(8):
                i = 8 * g + k
                lhs = jnp.concatenate([parts[i, 0], parts[i, 1]], axis=1)
                hi = jnp.concatenate([w_hi[2 * i, h], w_hi[2 * i + 1, h]], axis=0)
                lo = jnp.concatenate([w_lo[2 * i, h], w_lo[2 * i + 1, h]], axis=0)
                one = one + dot(lhs, hi, NN)
                two = two + dot(lhs[0:species], lo, NN)
            acc_s[:, at] = one
            acc2_s[:, at] = two
        return carry

    lax.fori_loop(0, rows // 16, gather, 0)
    held = acc_s[0:species] + acc_s[species:] + acc2_s[...]
    gas_at = held * inv_mass
    back_send[...] = jnp.transpose(
        jnp.concatenate([gas_at[:, :half], gas_at[:, half:]], axis=0)
    ).reshape(4, group, 2 * species)
    exchange(slab_row(back_send), slab_row(back_recv), back_ssem, back_rsem)

    await_all(base_recv, base_rsem)
    got = jnp.transpose(base_recv[...].reshape(half, 2 * species))
    base = jnp.concatenate([got[0:species], got[species:]], axis=1)
    emitted = base + emit_b[1, :, 0:1] * gas_at
    high, low = split(emitted)
    both = jnp.concatenate([high, low], axis=0)

    await_faces(second, 1)
    halo2 = merged(1)

    def last_step(x, carry):
        for k in range(ny // 2):
            i = x * (ny // 2) + k
            hi = jnp.concatenate(
                [jnp.concatenate([w_hi[2 * i + t, 0], w_hi[2 * i + t, 1]], axis=1) for t in range(2)], axis=0
            )
            lo = jnp.concatenate(
                [jnp.concatenate([w_lo[2 * i + t, 0], w_lo[2 * i + t, 1]], axis=1) for t in range(2)], axis=0
            )
            one = dot(both, hi, NT)
            add = one[0:species] + one[species:] + dot(high, lo, NT)
            for t in range(2):
                field = stencil(second, halo2, x, 2 * k + t) + add[:, t * cz:(t + 1) * cz]
                out_s[pl.ds(2 * i + t, species, stride=rows), :] = field
        return carry

    lax.fori_loop(0, nx, last_step, 0)

    await_all(back_recv, back_rsem)
    got = jnp.transpose(back_recv[...].reshape(half, 2 * species))
    seen = exact_dot(got, chosen, NN)
    seen = jnp.where(low_half, seen[0:species], seen[species:])
    for i in range(DROP_STEPS):
        drop[nodes - DROP_STEPS + i] = drop[nodes - DROP_STEPS + i] + reply_b[i] * seen

    await_all(meta_send.at[most], meta_ssem)
    await_all(base_send.at[:, most], base_ssem)
    await_all(back_send.at[:, most], back_ssem)
    drain_faces(first, 0)
    drain_faces(second, 1)


def store(gas, droplet, gas_out, drop_out, sem):
    copies = []
    for i, (src, dst) in enumerate(((gas, gas_out), (droplet, drop_out))):
        step = src.shape[0] // 4
        for k in range(4):
            at = pl.ds(k * step, step)
            copies.append(pltpu.make_async_copy(src.at[at], dst.at[at], sem.at[i, k]))
    for copy in copies:
        copy.start()
    for copy in copies:
        copy.wait()


def on_device(gas, droplet, owner, cells, weights, mass, liquid_rate, surface_rate, gas_rate):
    n_gx, n_gy, n_gz = (lax.axis_size(a) for a in ("gx", "gy", "gz"))
    species, nx, ny, cz = gas.shape
    nodes, _, parcels = droplet.shape
    group = n_gy * n_gz
    rows = nx * ny
    half = 4 * group
    vmem = pl.BlockSpec(memory_space=pltpu.VMEM)
    hbm = pl.BlockSpec(memory_space=pltpu.MemorySpace.HBM)
    dma = pltpu.SemaphoreType.DMA
    padded = pltpu.VMEM((nx + 2, ny + 2, species, cz), F32)
    slabs = pltpu.VMEM((4, group, 2 * species), F32)
    held = pltpu.VMEM((species, parcels), F32)
    onehot = pltpu.VMEM((rows, 2, cz, half), BF16)
    small = pltpu.VMEM((2, STENCIL, 8, half), F32)
    gas_next, droplet_next = pl.pallas_call(
        functools.partial(kernel, n_gx, n_gy, n_gz, nx, ny),
        out_shape=(
            jax.ShapeDtypeStruct((species * rows, cz), F32),
            jax.ShapeDtypeStruct(droplet.shape, F32),
        ),
        in_specs=[hbm] * 9,
        out_specs=(vmem, vmem),
        scratch_shapes=[
            pltpu.VMEM((1, parcels), jnp.int32), pltpu.VMEM((STENCIL, parcels), jnp.int32),
            pltpu.VMEM((STENCIL, parcels), F32), pltpu.VMEM((1, parcels), F32),
            pltpu.VMEM((1, species), F32), pltpu.VMEM((1, species), F32), pltpu.VMEM((1, species), F32),
            pltpu.VMEM((species * rows, cz), F32),
            padded, padded,
            pltpu.VMEM((rows // 2, 2, 2 * species, cz), BF16),
            held, held, pltpu.VMEM((species, cz), F32),
            pltpu.VMEM((DROP_STEPS, species, parcels), F32),
            pltpu.VMEM((2, species, parcels), F32),
            onehot, onehot, small, small, small, small,
            pltpu.VMEM((2 * species, 2 * half), F32),
            pltpu.VMEM((species, 2 * half), F32),
            pltpu.VMEM((group, 128), F32), pltpu.VMEM((group, 128), F32),
            slabs, slabs, slabs, slabs,
            pltpu.VMEM((2, species, cz), F32), pltpu.VMEM((2, 2, species, cz), F32),
            dma((2,)), dma((7,)),
            dma, dma, dma, dma, dma, dma,
            dma((2, 6)), dma((2, 6)),
        ],
        compiler_params=pltpu.CompilerParams(
            collective_id=0, has_side_effects=True, vmem_limit_bytes=40 << 20
        ),
        name="spray",
    )(*(
        pltpu.with_memory_space_constraint(a, pltpu.MemorySpace.HBM)
        for a in (
            gas.reshape(species * rows, cz), droplet, owner.reshape(1, parcels), cells, weights,
            mass.reshape(1, parcels), liquid_rate.reshape(1, species), surface_rate.reshape(1, species),
            gas_rate.reshape(1, species),
        )
    ))
    gas_next, droplet_next = pl.pallas_call(
        store,
        out_shape=(
            jax.ShapeDtypeStruct((species * rows, cz), F32),
            jax.ShapeDtypeStruct(droplet.shape, F32),
        ),
        in_specs=[vmem, vmem],
        out_specs=(hbm, hbm),
        scratch_shapes=[dma((2, 4))],
        name="store",
    )(*(
        pltpu.with_memory_space_constraint(a, pltpu.MemorySpace.VMEM) for a in (gas_next, droplet_next)
    ))
    return gas_next.reshape(gas.shape), droplet_next


def solution(mesh):
    return jax.shard_map(
        on_device,
        mesh=mesh,
        in_specs=(
            P(None, "gx", "gy", "gz"),
            P(None, None, ("gx", "gy", "gz")),
            P(("gx", "gy", "gz"), None),
            P(None, ("gx", "gy", "gz")),
            P(None, ("gx", "gy", "gz")),
            P(("gx", "gy", "gz")),
            P(),
            P(),
            P(),
        ),
        out_specs=(P(None, "gx", "gy", "gz"), P(None, None, ("gx", "gy", "gz"))),
        check_vma=False,
    )
```

```python
import functools

import jax
import jax.numpy as jnp
from jax import lax
from jax.experimental import pallas as pl
from jax.experimental.pallas import tpu as pltpu
from jax.sharding import PartitionSpec as P

STENCIL = 8
DROP_STEPS = 4
MESH = pl.DeviceIdType.MESH
F32 = jnp.float32
BF16 = jnp.bfloat16
EXACT = lax.Precision.HIGHEST
NT = (((1,), (1,)), ((), ()))
NN = (((1,), (0,)), ((), ()))


def iota(shape, dim):
    return lax.broadcasted_iota(jnp.int32, shape, dim)


def column(row, lanes=None):
    n = row.shape[1]
    spread = jnp.broadcast_to(row, (n, n))
    picked = jnp.where(iota((n, n), 0) == iota((n, n), 1), spread, jnp.zeros_like(spread))
    return jnp.sum(picked, axis=1, keepdims=True)


def split(value):
    high = value.astype(BF16)
    low = (value - high.astype(F32)).astype(BF16)
    return high, low


def exact_dot(a, b, dims):
    return lax.dot_general(a, b, dims, precision=EXACT, preferred_element_type=F32)


def dot(a, b, dims):
    return lax.dot_general(a, b, dims, preferred_element_type=F32)


def kernel(
    n_gx, n_gy, n_gz, nx, ny,
    gas, droplet, owner_in, cells_in, weights_in, mass_in, liquid_in, surface_in, gasrate_in,
    out_s, drop,
    owner, cells, weights, mass, liquid, surface, gasrate,
    raw, first, second, parts, lam_b, sig_b, gam_b, reply_b, emit_b,
    w_hi, w_lo, zk_s, rk_s, vh_s, vl_s, acc_s, acc2_s,
    meta_send, meta_recv, base_send, base_recv, back_send, back_recv,
    edge_send, edge_recv,
    in_sem, small_sem,
    meta_ssem, meta_rsem, base_ssem, base_rsem, back_ssem, back_rsem,
    face_ssem, face_rsem,
):
    group = n_gy * n_gz
    rows = nx * ny
    half = 4 * group
    species = liquid.shape[1]
    nodes = droplet.shape[0]
    parcels = owner.shape[1]
    cz = 128

    gx = lax.axis_index("gx")
    gy = lax.axis_index("gy")
    gz = lax.axis_index("gz")
    me = gy * n_gz + gz

    shifted_z = [lax.rem(gz + b, n_gz) for b in range(n_gz)]

    def each_peer(act):
        def turn(a, carry):
            to_y = lax.rem(gy + a, n_gy)
            for b in range(n_gz):
                to_z = shifted_z[b]
                run = functools.partial(act, to_y * n_gz + to_z, {"gy": to_y, "gz": to_z})
                if b == 0:
                    pl.when(a > 0)(run)
                else:
                    run()
            return carry

        lax.fori_loop(0, n_gy, turn, 0)

    smalls = [
        pltpu.make_async_copy(src, dst, small_sem.at[i])
        for i, (src, dst) in enumerate((
            (owner_in, owner), (cells_in, cells), (weights_in, weights), (mass_in, mass),
            (liquid_in, liquid), (surface_in, surface), (gasrate_in, gasrate),
        ))
    ]
    for copy in smalls:
        copy.start()
    gas_in = pltpu.make_async_copy(gas, raw, in_sem.at[0])
    gas_in.start()
    drop_in = pltpu.make_async_copy(droplet, drop, in_sem.at[1])
    drop_in.start()

    barrier = pltpu.get_barrier_semaphore()

    each_peer(lambda o, where: pl.semaphore_signal(
        barrier, inc=1, device_id=where, device_id_type=MESH
    ))
    for step in (1, n_gx - 1):
        pl.semaphore_signal(
            barrier, inc=1, device_id={"gx": lax.rem(gx + step, n_gx)}, device_id_type=MESH
        )

    for copy in smalls:
        copy.wait()
    own = owner[...]
    own_col = column(own)
    before = (own_col == own) & (iota((parcels, parcels), 0) < iota((parcels, parcels), 1))
    rank = jnp.sum(before.astype(F32), axis=0, keepdims=True).astype(jnp.int32)
    onehot = (iota((group, parcels), 0) == own).astype(F32)
    slot = (iota((8, parcels), 0) == rank).astype(F32)
    wts = weights[...]
    wts = wts / jnp.sum(wts, axis=0, keepdims=True)
    wts = wts * mass[...]
    cell = cells[...]
    cell_f = cell.astype(F32)
    tiles = [cell_f[q:q + 1] * slot for q in range(STENCIL)]
    tiles += [wts[q:q + 1] * slot for q in range(STENCIL)]
    spread = jnp.concatenate(tiles, axis=0)
    meta_send[...] = exact_dot(onehot, spread, NT)

    pl.semaphore_wait(barrier, group + 1)

    def exchange(src_of, dst_of, ssem, rsem):
        each_peer(lambda o, where: pltpu.make_async_remote_copy(
            src_ref=src_of(o), dst_ref=dst_of(me), send_sem=ssem, recv_sem=rsem,
            device_id=where, device_id_type=MESH,
        ).start())
        pltpu.make_async_copy(src_of(me), dst_of(me), rsem).start()

    def await_all(ref, sem):
        pltpu.make_async_copy(ref, ref, sem).wait()

    most = pl.ds(0, group - 1)

    meta_row = lambda ref: (lambda o: ref.at[pl.ds(o, 1)])
    slab_row = lambda ref: (lambda o: ref.at[:, pl.ds(o, 1)])

    exchange(meta_row(meta_send), meta_row(meta_recv), meta_ssem, meta_rsem)

    def faces(buf, step):
        inner_x, inner_y = pl.ds(1, nx), pl.ds(1, ny)
        table = [
            (gy > 0, {"gy": gy - 1}, buf.at[inner_x, 1], buf.at[inner_x, ny + 1], gy < n_gy - 1),
            (gy < n_gy - 1, {"gy": gy + 1}, buf.at[inner_x, ny], buf.at[inner_x, 0], gy > 0),
            (gz > 0, {"gz": gz - 1}, edge_send.at[step], edge_recv.at[step, 1], gz < n_gz - 1),
            (gz < n_gz - 1, {"gz": gz + 1}, edge_send.at[step], edge_recv.at[step, 0], gz > 0),
            (gx > 0, {"gx": gx - 1}, buf.at[1, inner_y], buf.at[nx + 1, inner_y], gx < n_gx - 1),
            (gx < n_gx - 1, {"gx": gx + 1}, buf.at[nx, inner_y], buf.at[0, inner_y], gx > 0),
        ]
        out = []
        for i, (send_if, target, src, dst, recv_if) in enumerate(table):
            copy = pltpu.make_async_remote_copy(
                src_ref=src, dst_ref=dst, send_sem=face_ssem.at[step, i],
                recv_sem=face_rsem.at[step, i], device_id=target, device_id_type=MESH,
            )
            out.append((send_if, copy, recv_if, dst))
        return out

    def start_faces(buf, step):
        for send_if, copy, _, _ in faces(buf, step):
            pl.when(send_if)(copy.start)

    def await_faces(buf, step):
        for i, (_, _, recv_if, dst) in enumerate(faces(buf, step)):
            wait = pltpu.make_async_copy(dst, dst, face_rsem.at[step, i]).wait
            pl.when(recv_if)(wait)

    def drain_faces(buf, step):
        for send_if, copy, _, _ in faces(buf, step):
            pl.when(send_if)(copy.wait_send)

    def outside_zero(buf, step):
        zero_x = jnp.zeros((ny, species, cz), F32)
        zero_y = jnp.zeros((nx, species, cz), F32)
        zero_z = jnp.zeros((species, cz), F32)

        @pl.when(gx == 0)
        def _():
            buf[0, 1:ny + 1] = zero_x

        @pl.when(gx == n_gx - 1)
        def _():
            buf[nx + 1, 1:ny + 1] = zero_x

        @pl.when(gy == 0)
        def _():
            buf[1:nx + 1, 0] = zero_y

        @pl.when(gy == n_gy - 1)
        def _():
            buf[1:nx + 1, ny + 1] = zero_y

        @pl.when(gz == 0)
        def _():
            edge_recv[step, 0] = zero_z

        @pl.when(gz == n_gz - 1)
        def _():
            edge_recv[step, 1] = zero_z

    lane = iota((species, cz), 1)
    def edge_part(field, r):
        return jnp.where(lane // 2 == r, pltpu.roll(field, 2 * r + 1, 1), 0.0)

    gas_in.wait()

    def load_rows(x, edges):
        for y in range(ny):
            r = x * ny + y
            field = raw[pl.ds(r, species, stride=rows), :]
            first[x + 1, y + 1] = field
            high, low = split(field)
            pair = x * (ny // 2) + y // 2
            parts[pair, y % 2, 0:species] = high
            parts[pair, y % 2, species:2 * species] = low
            edges = edges + edge_part(field, r)
        return edges

    edge_send[0] = lax.fori_loop(0, nx, load_rows, jnp.zeros((species, cz), F32))
    start_faces(first, 0)
    outside_zero(first, 0)
    outside_zero(second, 1)

    lam_b[...] = jnp.broadcast_to(column(liquid[...]), (species, parcels))
    sig_b[...] = jnp.broadcast_to(column(surface[...]), (species, parcels))
    gam_b[...] = jnp.broadcast_to(column(gasrate[...]), (species, cz))
    drop_in.wait()

    def droplet_block(b, carry):
        at = pl.ds(pl.multiple_of(b * 8, 8), 8)
        lam, sig = lam_b[at], sig_b[at]
        state = drop[:, at]
        unit = jnp.zeros((DROP_STEPS, 8, parcels), F32)
        base = jnp.zeros((8, parcels), F32)
        answer = jnp.zeros((8, parcels), F32)
        for _ in range(DROP_STEPS):
            flux = sig * state[-1]
            upper = jnp.concatenate([state[1:], state[-1:]], axis=0)
            lower = jnp.concatenate([state[1:2], state[:-1]], axis=0)
            state = state + lam[None] * (upper - 2.0 * state + lower)
            state = jnp.concatenate([state[:-1], (state[-1] - flux)[None]], axis=0)
            base = base + flux
            flux = sig * (unit[-1] - 1.0)
            upper = jnp.concatenate([unit[1:], unit[-1:]], axis=0)
            lower = jnp.concatenate([jnp.zeros_like(unit[:1]), unit[:-1]], axis=0)
            unit = unit + lam[None] * (upper - 2.0 * unit + lower)
            unit = jnp.concatenate([unit[:-1], (unit[-1] - flux)[None]], axis=0)
            answer = answer + flux
        drop[:, at] = state
        reply_b[:, at] = unit
        emit_b[0, at] = base
        emit_b[1, at] = answer
        return carry

    lax.fori_loop(0, species // 8, droplet_block, 0)
    place = lax.rem(rank, 4) * group + own
    chosen = (iota((half, parcels), 0) == place).astype(F32)
    low_half = rank < 4
    base = emit_b[0]
    base = jnp.concatenate([jnp.where(low_half, base, 0.0), jnp.where(low_half, 0.0, base)], axis=0)
    base_send[...] = exact_dot(chosen, base, NT).reshape(4, group, 2 * species)
    exchange(slab_row(base_send), slab_row(base_recv), base_ssem, base_rsem)

    await_all(meta_recv, meta_rsem)
    table = meta_recv[...]
    lane_slot = lax.rem(iota((group, 128), 1), 8)
    stacked = jnp.concatenate([jnp.where(lane_slot == j, table, 0.0) for j in range(8)], axis=0)
    gather_q = (iota((16, 128), 1) // 8 == iota((16, 128), 0)).astype(F32)
    byslot = exact_dot(gather_q, stacked, NT)
    ids = (byslot[0:STENCIL] + 0.5).astype(jnp.int32)
    vals = byslot[STENCIL:]
    total = vals
    for turn in range(1, STENCIL):
        same = pltpu.roll(ids, turn, 0) == ids
        total = total + jnp.where(same, pltpu.roll(vals, turn, 0), 0.0)
    sum_v = jnp.sum(vals, axis=0, keepdims=True)
    inv_mass = jnp.where(sum_v > 0.0, 1.0 / jnp.where(sum_v > 0.0, sum_v, 1.0), 0.0)
    r_f = (ids // cz).astype(F32)
    z_f = lax.rem(ids, cz).astype(F32)
    v_high = total.astype(BF16).astype(F32)
    v_low = total - v_high
    for h in range(2):
        for k in range(STENCIL):
            for ref, val in ((zk_s, z_f), (rk_s, r_f), (vh_s, v_high), (vl_s, v_low)):
                one = val[k:k + 1, h * half:(h + 1) * half]
                ref[h, k] = jnp.broadcast_to(one, (8, half))

    zero = jnp.zeros((16, half), BF16)

    def twice(value):
        return jnp.concatenate([value, value], axis=0).astype(BF16)

    def build_row(h, r):
        at_row = jnp.full((8, half), r.astype(F32))
        key = [twice(jnp.where(rk_s[h, k] == at_row, zk_s[h, k], -1.0)) for k in range(STENCIL)]
        vh = [twice(vh_s[h, k]) for k in range(STENCIL)]
        vl = [twice(vl_s[h, k]) for k in range(STENCIL)]
        for chunk in range(cz // 16):
            z = (iota((16, half), 0) + chunk * 16).astype(F32).astype(BF16)
            high, low = zero, zero
            for k in reversed(range(STENCIL)):
                hit = key[k] == z
                high = jnp.where(hit, vh[k], high)
                low = jnp.where(hit, vl[k], low)
            w_hi[r, h, chunk * 16:chunk * 16 + 16] = high
            w_lo[r, h, chunk * 16:chunk * 16 + 16] = low

    def build(h, i, carry):
        build_row(h, 2 * i)
        build_row(h, 2 * i + 1)
        return carry

    def merged(step):
        up = edge_recv[step, 1]
        down = edge_recv[step, 0]
        even = lax.rem(lane, 2) == 0
        return jnp.where(even, pltpu.roll(up, cz - 1, 1), pltpu.roll(down, 1, 1))

    def stencil(buf, halo, x, y):
        r = x * ny + y
        x, y = x + 1, y + 1
        mid = buf[x, y]
        beside = buf[x + 1, y] + buf[x - 1, y]
        beside = beside + buf[x, y + 1] + buf[x, y - 1]
        ends = pltpu.roll(halo, cz - 1 - 2 * r, 1)
        beside = beside + jnp.where(lane == cz - 1, ends, pltpu.roll(mid, cz - 1, 1))
        beside = beside + jnp.where(lane == 0, ends, pltpu.roll(mid, 1, 1))
        return mid + gam_b[...] * (beside - 6.0 * mid)

    await_faces(first, 0)
    halo = merged(0)

    def first_step(x, edges):
        for y in range(ny):
            field = stencil(first, halo, x, y)
            second[x + 1, y + 1] = field
            edges = edges + edge_part(field, x * ny + y)
        return edges

    edge_send[1] = lax.fori_loop(0, nx, first_step, jnp.zeros((species, cz), F32))
    start_faces(second, 1)
    lax.fori_loop(0, rows // 2, functools.partial(build, 0), 0)


    lax.fori_loop(0, rows // 2, functools.partial(build, 1), 0)

    acc_s[...] = jnp.zeros_like(acc_s)
    acc2_s[...] = jnp.zeros_like(acc2_s)

    def gather(g, carry):
        for h in range(2):
            at = slice(h * half, (h + 1) * half)
            one, two = acc_s[:, at], acc2_s[:, at]
            for k in range(8):
                i = 8 * g + k
                lhs = jnp.concatenate([parts[i, 0], parts[i, 1]], axis=1)
                hi = jnp.concatenate([w_hi[2 * i, h], w_hi[2 * i + 1, h]], axis=0)
                lo = jnp.concatenate([w_lo[2 * i, h], w_lo[2 * i + 1, h]], axis=0)
                one = one + dot(lhs, hi, NN)
                two = two + dot(lhs[0:species], lo, NN)
            acc_s[:, at] = one
            acc2_s[:, at] = two
        return carry

    lax.fori_loop(0, rows // 16, gather, 0)
    held = acc_s[0:species] + acc_s[species:] + acc2_s[...]
    gas_at = held * inv_mass
    back_send[...] = jnp.transpose(
        jnp.concatenate([gas_at[:, :half], gas_at[:, half:]], axis=0)
    ).reshape(4, group, 2 * species)
    exchange(slab_row(back_send), slab_row(back_recv), back_ssem, back_rsem)

    await_all(base_recv, base_rsem)
    got = jnp.transpose(base_recv[...].reshape(half, 2 * species))
    base = jnp.concatenate([got[0:species], got[species:]], axis=1)
    emitted = base + emit_b[1, :, 0:1] * gas_at
    high, low = split(emitted)
    both = jnp.concatenate([high, low], axis=0)

    await_faces(second, 1)
    halo2 = merged(1)

    def last_step(x, carry):
        for k in range(ny // 2):
            i = x * (ny // 2) + k
            hi = jnp.concatenate(
                [jnp.concatenate([w_hi[2 * i + t, 0], w_hi[2 * i + t, 1]], axis=1) for t in range(2)], axis=0
            )
            lo = jnp.concatenate(
                [jnp.concatenate([w_lo[2 * i + t, 0], w_lo[2 * i + t, 1]], axis=1) for t in range(2)], axis=0
            )
            one = dot(both, hi, NT)
            add = one[0:species] + one[species:] + dot(high, lo, NT)
            for t in range(2):
                field = stencil(second, halo2, x, 2 * k + t) + add[:, t * cz:(t + 1) * cz]
                out_s[pl.ds(2 * i + t, species, stride=rows), :] = field
        return carry

    lax.fori_loop(0, nx, last_step, 0)

    await_all(back_recv, back_rsem)
    got = jnp.transpose(back_recv[...].reshape(half, 2 * species))
    seen = exact_dot(got, chosen, NN)
    seen = jnp.where(low_half, seen[0:species], seen[species:])
    for i in range(DROP_STEPS):
        drop[nodes - DROP_STEPS + i] = drop[nodes - DROP_STEPS + i] + reply_b[i] * seen

    await_all(meta_send.at[most], meta_ssem)
    await_all(base_send.at[:, most], base_ssem)
    await_all(back_send.at[:, most], back_ssem)
    drain_faces(first, 0)
    drain_faces(second, 1)


def store(gas, droplet, gas_out, drop_out, sem):
    copies = []
    for i, (src, dst) in enumerate(((gas, gas_out), (droplet, drop_out))):
        step = src.shape[0] // 2
        for k in range(2):
            at = pl.ds(k * step, step)
            copies.append(pltpu.make_async_copy(src.at[at], dst.at[at], sem.at[i, k]))
    for copy in copies:
        copy.start()
    for copy in copies:
        copy.wait()


def on_device(gas, droplet, owner, cells, weights, mass, liquid_rate, surface_rate, gas_rate):
    n_gx, n_gy, n_gz = (lax.axis_size(a) for a in ("gx", "gy", "gz"))
    species, nx, ny, cz = gas.shape
    nodes, _, parcels = droplet.shape
    group = n_gy * n_gz
    rows = nx * ny
    half = 4 * group
    vmem = pl.BlockSpec(memory_space=pltpu.VMEM)
    hbm = pl.BlockSpec(memory_space=pltpu.MemorySpace.HBM)
    dma = pltpu.SemaphoreType.DMA
    padded = pltpu.VMEM((nx + 2, ny + 2, species, cz), F32)
    slabs = pltpu.VMEM((4, group, 2 * species), F32)
    held = pltpu.VMEM((species, parcels), F32)
    onehot = pltpu.VMEM((rows, 2, cz, half), BF16)
    small = pltpu.VMEM((2, STENCIL, 8, half), F32)
    gas_next, droplet_next = pl.pallas_call(
        functools.partial(kernel, n_gx, n_gy, n_gz, nx, ny),
        out_shape=(
            jax.ShapeDtypeStruct((species * rows, cz), F32),
            jax.ShapeDtypeStruct(droplet.shape, F32),
        ),
        in_specs=[hbm] * 9,
        out_specs=(vmem, vmem),
        scratch_shapes=[
            pltpu.VMEM((1, parcels), jnp.int32), pltpu.VMEM((STENCIL, parcels), jnp.int32),
            pltpu.VMEM((STENCIL, parcels), F32), pltpu.VMEM((1, parcels), F32),
            pltpu.VMEM((1, species), F32), pltpu.VMEM((1, species), F32), pltpu.VMEM((1, species), F32),
            pltpu.VMEM((species * rows, cz), F32),
            padded, padded,
            pltpu.VMEM((rows // 2, 2, 2 * species, cz), BF16),
            held, held, pltpu.VMEM((species, cz), F32),
            pltpu.VMEM((DROP_STEPS, species, parcels), F32),
            pltpu.VMEM((2, species, parcels), F32),
            onehot, onehot, small, small, small, small,
            pltpu.VMEM((2 * species, 2 * half), F32),
            pltpu.VMEM((species, 2 * half), F32),
            pltpu.VMEM((group, 128), F32), pltpu.VMEM((group, 128), F32),
            slabs, slabs, slabs, slabs,
            pltpu.VMEM((2, species, cz), F32), pltpu.VMEM((2, 2, species, cz), F32),
            dma((2,)), dma((7,)),
            dma, dma, dma, dma, dma, dma,
            dma((2, 6)), dma((2, 6)),
        ],
        compiler_params=pltpu.CompilerParams(
            collective_id=0, has_side_effects=True, vmem_limit_bytes=40 << 20
        ),
        name="spray",
    )(*(
        pltpu.with_memory_space_constraint(a, pltpu.MemorySpace.HBM)
        for a in (
            gas.reshape(species * rows, cz), droplet, owner.reshape(1, parcels), cells, weights,
            mass.reshape(1, parcels), liquid_rate.reshape(1, species), surface_rate.reshape(1, species),
            gas_rate.reshape(1, species),
        )
    ))
    gas_next, droplet_next = pl.pallas_call(
        store,
        out_shape=(
            jax.ShapeDtypeStruct((species * rows, cz), F32),
            jax.ShapeDtypeStruct(droplet.shape, F32),
        ),
        in_specs=[vmem, vmem],
        out_specs=(hbm, hbm),
        scratch_shapes=[dma((2, 2))],
        name="store",
    )(*(
        pltpu.with_memory_space_constraint(a, pltpu.MemorySpace.VMEM) for a in (gas_next, droplet_next)
    ))
    return gas_next.reshape(gas.shape), droplet_next


def solution(mesh):
    return jax.shard_map(
        on_device,
        mesh=mesh,
        in_specs=(
            P(None, "gx", "gy", "gz"),
            P(None, None, ("gx", "gy", "gz")),
            P(("gx", "gy", "gz"), None),
            P(None, ("gx", "gy", "gz")),
            P(None, ("gx", "gy", "gz")),
            P(("gx", "gy", "gz")),
            P(),
            P(),
            P(),
        ),
        out_specs=(P(None, "gx", "gy", "gz"), P(None, None, ("gx", "gy", "gz"))),
        check_vma=False,
    )
```
